256 devices in a mesh: group: 32 (over y, z), pencil: 8 (over x, core).
Axes of the slice: x: 4, y: 4, z: 8, core: 2. Of those that a mesh axis runs over, the one named last changes fastest.
Arguments:
- mult_iterate: float32 [32, 8, 8192], P('group', 'pencil'), may hold values from -6 to 6
- residual: float32 [32, 8, 8192], P('group', 'pencil'), may hold values from -6 to 6
- direction: float32 [32, 8, 8192], P('group', 'pencil'), may hold values from -6 to 6
- mult_scale: float32 [32, 8, 8192], P('group', 'pencil'), may hold values from 0.5 to 18
- eigen_basis: float32 [128, 3, 64, 64], P('group'), may hold values from -1 to 1
- eigen_values: float32 [128, 3, 64], P('group'), may hold values from 0.2 to 2
- elastic_coef: float32 [128, 3, 3], P('group'), may hold values from 0.5 to 2
- coarse_inverse: float32 [1024, 1024], replicated, may hold values from -1 to 2.5
- send_pos: int32 [32, 8, 16384], P('group', 'pencil'), may hold values from 0 to 24191, as said below
- pair_slots: int32 [32, 8, 2, 8192], P('group', 'pencil'), may hold values from 0 to 16383, as said below
- prim_rows: int32 [32, 8, 32], P('group', 'pencil'), may hold values from 0 to 16383, as said below
- coarse_idx: int32 [32, 8, 32], P('group', 'pencil'), may hold values from 0 to 1023
Outputs:
- new_iterate: float32 [32, 8, 8192], P('group', 'pencil')
- new_residual: float32 [32, 8, 8192], P('group', 'pencil')
- new_direction: float32 [32, 8, 8192], P('group', 'pencil')
The draws below stay inside these ranges and needn't reach their ends.
Inputs may be any that keep to these rules, and one draw needn't show every extreme that they name: `send_pos`: distinct within each block (g, s). `pair_slots`: in each block (g, s) the two rows together hold every number of 0 to 16383 once. `prim_rows`: distinct within each block (g, s).
All inputs are finite; a program needn't handle non-finite values.
Results may differ from the reference program's by a relative error of at most 0.0003.
Values sent between devices are 32-bit elements; how exact they have to be, the bound alone decides.
No kernel may reach another device: no remote copies, remote signals or barrier semaphores. Data moves between devices by JAX's collectives and lax.ppermute only.
A program may use at most 128 MiB of HBM per device.

```python
import math
import jax
import jax.numpy as jnp
from jax import lax

N = 64
C = 3
PG = 4
IFD = 16384
PRIM_DEV = 32
XS = 8
SHARE = 512
MULT_DEV = 8192
NPAT = 128
NC = 1024
N_GROUP = 32
N_PENCIL = 8


def draw_send_pos(key, part):
    face_count = XS * PG * C * (4 * N - 4)
    blocks = N_GROUP * N_PENCIL

    def one_block(block_key):
        interior = jax.random.permutation(block_key, face_count - 2).astype(jnp.int32) + 1
        chosen = jnp.concatenate([jnp.array([0, face_count - 1], jnp.int32), interior[:IFD - 2]])
        shuffle = jax.random.permutation(jax.random.fold_in(block_key, 7), IFD)
        return chosen[shuffle]
    picked = jax.vmap(one_block)(jax.random.split(key, blocks))
    return picked.reshape(N_GROUP, N_PENCIL, IFD).astype(jnp.int32)


def draw_pair_slots(key, part):
    blocks = N_GROUP * N_PENCIL

    def one_block(block_key):
        return jax.random.permutation(block_key, IFD).astype(jnp.int32).reshape(MULT_DEV, 2).T
    picked = jax.vmap(one_block)(jax.random.split(key, blocks))
    return picked.reshape(N_GROUP, N_PENCIL, 2, MULT_DEV)


def draw_prim_rows(key, part):
    blocks = N_GROUP * N_PENCIL

    def one_block(block_key):
        interior = jax.random.permutation(block_key, IFD - 2).astype(jnp.int32) + 1
        chosen = jnp.concatenate([jnp.array([0, IFD - 1], jnp.int32), interior[:PRIM_DEV - 2]])
        shuffle = jax.random.permutation(jax.random.fold_in(block_key, 11), PRIM_DEV)
        return chosen[shuffle]
    picked = jax.vmap(one_block)(jax.random.split(key, blocks))
    return picked.reshape(N_GROUP, N_PENCIL, PRIM_DEV)


def draw_mult_scale(key, part):
    shape = (N_GROUP, N_PENCIL, MULT_DEV)
    base_scale = jnp.exp(jax.random.uniform(key, shape, jnp.float32, math.log(0.5), math.log(2.0)))
    device = (jnp.arange(N_GROUP)[:, None] * N_PENCIL + jnp.arange(N_PENCIL)[None, :]).astype(jnp.float32)
    fraction = device / max(N_GROUP * N_PENCIL - 1, 1)
    growth = 3.0
    return base_scale * jnp.power(growth, fraction)[:, :, None]


def draw_eigen_basis(key, part):
    shape = (NPAT, 3, N, N)
    noise = jax.random.uniform(key, shape, jnp.float32, -1.0, 1.0)
    identity = jnp.eye(N, dtype=jnp.float32)
    return identity + noise * (0.5 / N) * (1.0 - identity)


def draw_coarse_inverse(key, part):
    noise = jax.random.uniform(key, (NC, NC), jnp.float32, -1.0, 1.0)
    mirror = 0.5 * (noise + noise.T)
    offdiag = jnp.cbrt(mirror) * (0.9 / NC)
    diagonal = jnp.exp(jax.random.uniform(jax.random.fold_in(key, 5), (NC,), jnp.float32, 0.0, math.log(2.5)))
    identity = jnp.eye(NC, dtype=jnp.float32)
    return offdiag * (1.0 - identity) + identity * diagonal[:, None]


def place_ends(drawn, own_key, low, high):
    shape = drawn.shape
    spot = [jax.random.randint(jax.random.fold_in(own_key, axis), (), 0, shape[axis]) for axis in range(len(shape))]
    drawn = drawn.at[tuple(spot)].set(low)
    longest = shape.index(max(shape))
    spot[longest] = (spot[longest] + 1) % shape[longest]
    return drawn.at[tuple(spot)].set(high)


def levels(stream_key, shape, shards, least, top_value):
    level = 1.0
    for dim, shards_of in shards:
        heights = jax.random.uniform(jax.random.fold_in(jax.random.fold_in(stream_key, 6), dim), (shards_of,), jnp.float32, least / len(shards), top_value / len(shards))
        level = level * jnp.repeat(jnp.exp(heights), shape[dim] // shards_of).reshape((-1,) + (1,) * (len(shape) - 1 - dim))
    return level


def bell_draw(stream_key, dims, width, limit, shards=(), kind=jnp.bfloat16):
    values = width * jax.random.normal(stream_key, dims, jnp.float32)
    if shards:
        values = values * levels(stream_key, dims, shards, -0.22, 0.18)
    return jnp.clip(values, -limit, limit).astype(kind)


def setup_inputs(seed: int = 0) -> dict:
    seeds = jax.random.split(jax.random.key(seed), 13)
    return {
        "mult_iterate": bell_draw(seeds[0], (N_GROUP, N_PENCIL, MULT_DEV), 1.0, 6.0, ((0, 32), (1, 8)), jnp.float32),
        "residual": bell_draw(seeds[1], (N_GROUP, N_PENCIL, MULT_DEV), 1.0, 6.0, ((0, 32), (1, 8)), jnp.float32),
        "direction": bell_draw(seeds[2], (N_GROUP, N_PENCIL, MULT_DEV), 1.0, 6.0, ((0, 32), (1, 8)), jnp.float32),
        "mult_scale": draw_mult_scale(jax.random.fold_in(seeds[12], 71), 0),
        "eigen_basis": draw_eigen_basis(jax.random.fold_in(seeds[12], 71), 0),
        "eigen_values": jnp.clip(jnp.exp(math.log(2.0) - 2.3025851 * jax.random.uniform(seeds[5], (NPAT, 3, N), jnp.float32) ** levels(seeds[5], (NPAT, 3, N), ((0, 32),), -0.2, 0.2)), 0.2, 2.0),
        "elastic_coef": jnp.clip(jnp.exp(math.log(2.0) - 1.3862944 * jax.random.uniform(seeds[6], (NPAT, C, 3), jnp.float32) ** levels(seeds[6], (NPAT, C, 3), ((0, 32),), -0.2, 0.2)), 0.5, 2.0),
        "coarse_inverse": draw_coarse_inverse(jax.random.fold_in(seeds[12], 71), 0),
        "send_pos": draw_send_pos(jax.random.fold_in(seeds[12], 71), 0),
        "pair_slots": draw_pair_slots(jax.random.fold_in(seeds[12], 71), 0),
        "prim_rows": draw_prim_rows(jax.random.fold_in(seeds[12], 71), 0),
        "coarse_idx": place_ends(jax.random.randint(seeds[11], (N_GROUP, N_PENCIL, PRIM_DEV), 0, NC), jax.random.fold_in(seeds[11], 1), 0, NC - 1).astype(jnp.int32),
    }


def face_to_flat(index, extent):
    cycle_size = 4 * extent - 4
    plane_index = index // cycle_size
    cycle_spot = index % cycle_size
    y_index = jnp.where(cycle_spot < extent, 0, jnp.where(cycle_spot < 2 * extent - 2, cycle_spot - extent + 1, jnp.where(cycle_spot < 3 * extent - 4, cycle_spot - (2 * extent - 2) + 1, extent - 1)))
    z_index = jnp.where(cycle_spot < extent, cycle_spot, jnp.where(cycle_spot < 2 * extent - 2, 0, jnp.where(cycle_spot < 3 * extent - 4, extent - 1, cycle_spot - (3 * extent - 4))))
    return (plane_index * extent * extent + y_index * extent + z_index).astype(jnp.int32)


def spectrum(coeffs, along_x, along_y, along_z):
    first = coeffs[None, :, :, 0, None, None] * along_x.T[:, :, None, None, None]
    second = coeffs[None, :, :, 1, None, None] * along_y[None, :, None, :, None]
    third = coeffs[None, :, :, 2, None, None] * along_z[None, :, None, None, :]
    return first + second + third


def transform_in(volume, basis):
    highest = lax.Precision.HIGHEST
    step_one = jnp.einsum('xpcyz,pzk->xpcyk', volume, basis[:, 2], precision=highest)
    step_two = jnp.einsum('xpcyk,pyj->xpcjk', step_one, basis[:, 1], precision=highest)
    return jnp.einsum('xpcjk,pxi->ipcjk', step_two, basis[:, 0], precision=highest)


def transform_out(volume, basis):
    highest = lax.Precision.HIGHEST
    step_one = jnp.einsum('ipcjk,pxi->xpcjk', volume, basis[:, 0], precision=highest)
    step_two = jnp.einsum('xpcjk,pyj->xpcyk', step_one, basis[:, 1], precision=highest)
    return jnp.einsum('xpcyk,pzk->xpcyz', step_two, basis[:, 2], precision=highest)


def place_slab(row_values, row_positions):
    slab_size = XS * PG * C * N * N
    return jnp.zeros((slab_size,), jnp.float32).at[row_positions].set(row_values)


def place_back(search_row, pair_row):
    return jnp.zeros((IFD,), jnp.float32).at[pair_row[0]].set(search_row).at[pair_row[1]].set(-search_row)


def add_primal(values_row, primal_row, coarse_row, lifted):
    return values_row.at[primal_row].add(lifted[coarse_row])


def group_solve(pieces):
    rows_group, positions_group, basis_group, values_group, coeffs_group = pieces
    slabs = jax.vmap(place_slab)(rows_group, positions_group)
    volume = slabs.reshape(N, PG, C, N, N)
    spectral = transform_in(volume, basis_group)
    scaled = spectral / spectrum(coeffs_group, values_group[:, 0], values_group[:, 1], values_group[:, 2])
    displace = transform_out(scaled, basis_group).reshape(N_PENCIL, XS * PG * C * N * N)
    return jnp.take_along_axis(displace, positions_group, axis=1)


def reference(mult_iterate, residual, direction, mult_scale, eigen_basis, eigen_values, elastic_coef, coarse_inverse, send_pos, pair_slots, prim_rows, coarse_idx):
    highest = lax.Precision.HIGHEST
    flat_pos = face_to_flat(send_pos, N)
    back = jax.vmap(jax.vmap(place_back))(direction, pair_slots)
    rows = back.reshape(N_GROUP, N_PENCIL, N_GROUP, SHARE).transpose(2, 1, 0, 3).reshape(N_GROUP, N_PENCIL, IFD)
    picked = lax.map(group_solve, (rows, flat_pos, eigen_basis.reshape(N_GROUP, PG, 3, N, N), eigen_values.reshape(N_GROUP, PG, 3, N), elastic_coef.reshape(N_GROUP, PG, C, 3)))
    primal_values = jnp.take_along_axis(picked, prim_rows, axis=2)
    coarse = jax.ops.segment_sum(primal_values.reshape(-1), coarse_idx.reshape(-1), num_segments=NC)
    lifted = jnp.dot(coarse_inverse, coarse, precision=highest)
    sent = jax.vmap(jax.vmap(add_primal, in_axes=(0, 0, 0, None)), in_axes=(0, 0, 0, None))(picked, prim_rows, coarse_idx, lifted)
    arrived = sent.reshape(N_GROUP, N_PENCIL, N_GROUP, SHARE).transpose(2, 1, 0, 3).reshape(N_GROUP, N_PENCIL, IFD)
    image = jnp.take_along_axis(arrived, pair_slots[:, :, 0], axis=2) - jnp.take_along_axis(arrived, pair_slots[:, :, 1], axis=2)
    old = jnp.sum(residual * mult_scale * residual)
    step_size = old / jnp.sum(direction * image)
    new_iterate = mult_iterate + step_size * direction
    new_residual = residual - step_size * image
    precond = mult_scale * new_residual
    new_norm = jnp.sum(new_residual * precond)
    new_direction = precond + (new_norm / old) * direction
    return (new_iterate, new_residual, new_direction)
```

```python
import functools

import jax
import jax.numpy as jnp
from jax import lax
from jax.experimental import pallas as pl
from jax.experimental.pallas import tpu as pltpu
from jax.sharding import PartitionSpec as P

LANES = 128
BF16 = jnp.bfloat16
F32 = jnp.float32
HIGHEST = lax.Precision.HIGHEST
VMEM = pl.BlockSpec(memory_space=pltpu.VMEM)


def call(kernel, out_shape, count, name, scratch=(), flops=1_000_000):
    single = not isinstance(out_shape, (tuple, list))
    return pl.pallas_call(
        kernel,
        out_shape=out_shape,
        in_specs=[VMEM] * count,
        out_specs=VMEM if single else [VMEM] * len(out_shape),
        scratch_shapes=list(scratch),
        name=name,
        cost_estimate=pl.CostEstimate(flops=flops, bytes_accessed=1 << 18, transcendentals=0),
    )


def split_channels(value, count):
    pieces = []
    for _ in range(count):
        piece = value.astype(BF16).astype(F32)
        pieces.append(piece)
        value = value - piece
    return pieces


def scatter_rows(rows, high_row, low_row, piece_rows, chunk, total, channels):
    row_ids = lax.broadcasted_iota(jnp.int32, (rows, LANES), 0).astype(F32).astype(BF16)
    lane_ids = lax.broadcasted_iota(jnp.int32, (LANES, LANES), 0).astype(F32).astype(BF16)

    def step(index, acc):
        left, right = [], []
        for r in range(chunk):
            high = jnp.broadcast_to(high_row(index, r), (rows, LANES)).astype(BF16)
            low = jnp.broadcast_to(low_row(index, r), (LANES, LANES)).astype(BF16)
            left.append(jnp.where(row_ids == high, BF16(1), BF16(0)))
            match = lane_ids == low
            right.append(
                jnp.concatenate(
                    [
                        jnp.where(
                            match,
                            jnp.broadcast_to(piece_rows(c, index, r), (LANES, LANES)).astype(BF16),
                            BF16(0),
                        )
                        for c in range(channels)
                    ],
                    axis=0,
                )
            )
        left = jnp.concatenate(left, axis=1)
        right = jnp.concatenate(right, axis=1)
        return acc + lax.dot_general(
            left, right, (((1,), (1,)), ((), ())), preferred_element_type=F32
        )

    acc = jnp.zeros((rows, LANES * channels), F32)
    if total == chunk:
        acc = step(0, acc)
    else:
        acc = lax.fori_loop(0, total // chunk, step, acc)
    out = acc[:, :LANES]
    for c in range(1, channels):
        out = out + acc[:, c * LANES : (c + 1) * LANES]
    return out


def gather_block(indices, table_row, table_rows, chains=4):
    high = lax.shift_right_arithmetic(indices, 7)
    low = jnp.bitwise_and(indices, LANES - 1)
    acc = [jnp.zeros(indices.shape, F32) for _ in range(chains)]
    for a in range(table_rows):
        row = jnp.broadcast_to(table_row(a), indices.shape)
        picked = jnp.take_along_axis(row, low, axis=1, mode="promise_in_bounds")
        acc[a % chains] = jnp.where(high == a, picked, acc[a % chains])
    out = acc[0]
    for other in acc[1:]:
        out = out + other
    return out


def split_index(idx_ref, high_ref, low_ref):
    idx = idx_ref[...]
    high_ref[...] = lax.shift_right_arithmetic(idx, 7).astype(F32)
    low_ref[...] = jnp.bitwise_and(idx, LANES - 1).astype(F32)


CHUNK = 16


def back_kernel(idx_ref, dir_ref, extra_ref, out_ref, high_ref, low_ref, piece_ref, acc_ref):
    split_index(idx_ref, high_ref, low_ref)
    half = dir_ref.shape[0]
    for c, piece in enumerate(split_channels(dir_ref[...], 2)):
        piece_ref[c, :half, :] = piece
        piece_ref[c, half:, :] = -piece
    rows = idx_ref.shape[0]
    acc_ref[...] = scatter_rows(
        rows,
        lambda t, r: high_ref[pl.ds(t * CHUNK + r, 1), :],
        lambda t, r: low_ref[pl.ds(t * CHUNK + r, 1), :],
        lambda c, t, r: piece_ref[c, pl.ds(t * CHUNK + r, 1), :],
        CHUNK,
        rows,
        2,
    )
    for h in range(out_ref.shape[0]):
        out_ref[h, 0:4, :] = acc_ref[4 * h : 4 * h + 4, :]
        out_ref[h, 4:8, :] = extra_ref[0:4, :]


def load_kernel(arr_ref, idx_ref, out_ref, high_ref, low_ref, piece_ref, acc_ref):
    split_index(idx_ref, high_ref, low_ref)
    rows = idx_ref.shape[0]
    groups = arr_ref.shape[0]
    values = arr_ref[...].reshape(groups * 8, LANES)
    for c, piece in enumerate(split_channels(values, 2)):
        piece_ref[c] = piece
    table = acc_ref.shape[0]
    acc_ref[...] = scatter_rows(
        table,
        lambda t, r: high_ref[pl.ds(t * CHUNK + r, 1), :],
        lambda t, r: low_ref[pl.ds(t * CHUNK + r, 1), :],
        lambda c, t, r: piece_ref[c, pl.ds(t * CHUNK * 2 + (r // 4) * 8 + r % 4, 1), :],
        CHUNK,
        rows,
        2,
    )
    for dest in range(out_ref.shape[0]):
        for half in range(2):
            start = (dest // 2) * 48 + half * 24
            out_ref[dest, :, half * LANES : (half + 1) * LANES] = acc_ref[start : start + 24, :]


def full_dot(left, right, contract):
    return lax.dot_general(
        left, right, ((contract[0], contract[1]), ((), ())), precision=HIGHEST,
        preferred_element_type=F32,
    )


def solve_kernel(
    recv_ref, bxt_ref, bx_ref, bdt_ref, bd_ref, cst_ref, out_ref, fwd_ref, d0_ref, d1_ref
):
    sources = recv_ref.shape[0]
    load = jnp.concatenate(
        [recv_ref[src, 8 * c : 8 * c + 8, :] for c in range(3) for src in range(sources)], axis=0
    )
    along_x = full_dot(bxt_ref[...], load, ((1,), (0,)))
    fwd_ref[...] = full_dot(bdt_ref[...], along_x, ((1,), (1,)))

    def step(j, carry):
        top, bottom = carry

        def row(index):
            return jnp.broadcast_to(cst_ref[index, pl.ds(j, 1), :], (64, LANES))

        first = jnp.broadcast_to(fwd_ref[pl.ds(64 + j, 1), :], (64, LANES))
        last = jnp.broadcast_to(fwd_ref[pl.ds(128 + j, 1), :], (64, LANES))
        y_first, y_last = row(0), row(1)
        spectral = (
            y_first * fwd_ref[0:64, :]
            + y_last * fwd_ref[192:256, :]
            + first * cst_ref[2]
            + last * cst_ref[3]
        )
        scaled = spectral / (row(4) + cst_ref[5])
        along_first = cst_ref[2] * scaled
        along_last = cst_ref[3] * scaled
        d0_ref[j] = jnp.sum(along_first.reshape(8, 8, LANES), axis=0)
        d1_ref[j] = jnp.sum(along_last.reshape(8, 8, LANES), axis=0)
        return top + y_first * scaled, bottom + y_last * scaled

    zero = jnp.zeros((64, LANES), F32)
    top, bottom = lax.fori_loop(0, 64, step, (zero, zero), unroll=4)
    edges = jnp.concatenate(
        [top, jnp.sum(d0_ref[...], axis=1), jnp.sum(d1_ref[...], axis=1), bottom], axis=0
    )
    cells = full_dot(bd_ref[...], edges, ((1,), (0,)))
    slabs = full_dot(bx_ref[...], cells, ((1,), (1,)))
    for c in range(3):
        for dest in range(out_ref.shape[0]):
            out_ref[dest, 8 * c : 8 * c + 8, :] = slabs[
                64 * c + 8 * dest : 64 * c + 8 * dest + 8, :
            ]


def pick_kernel(recv_ref, idx_ref, out_ref, table_ref, pick_ref):
    for p in range(recv_ref.shape[0] // 2):
        for half in range(2):
            lanes = slice(half * LANES, (half + 1) * LANES)
            start = p * 48 + half * 24
            table_ref[start : start + 24, :] = (
                recv_ref[2 * p, :, lanes] + recv_ref[2 * p + 1, :, lanes]
            )
    table_rows = table_ref.shape[0]

    def table_row(a):
        return table_ref[a : a + 1, :]

    def block(t, carry):
        start = pl.multiple_of(t * 16, 16)
        pick_ref[pl.ds(start, 16), :] = gather_block(
            idx_ref[pl.ds(start, 16), :], table_row, table_rows, 2
        )
        return carry

    lax.fori_loop(0, 9, block, 0)
    primal = pick_ref[128:132, :]
    for h in range(out_ref.shape[0]):
        out_ref[h, 0:4, :] = pick_ref[4 * h : 4 * h + 4, :]
        out_ref[h, 4:8, :] = primal


def coarse_kernel(arr_ref, ids_ref, out_ref, high_ref, low_ref, piece_ref):
    split_index(ids_ref, high_ref, low_ref)
    packed = []
    for q in range(8):
        row = arr_ref[4 * q, 4:5, :]
        for step in range(1, 4):
            row = row + arr_ref[4 * q + step, 4:5, :]
        packed.append(row)
    for c, piece in enumerate(split_channels(jnp.concatenate(packed, axis=0), 3)):
        piece_ref[c] = piece
    partial = scatter_rows(
        16,
        lambda t, r: high_ref[pl.ds(r, 1), :],
        lambda t, r: low_ref[pl.ds(r, 1), :],
        lambda c, t, r: piece_ref[c, pl.ds(r, 1), :],
        8,
        8,
        3,
    )
    for dest in range(out_ref.shape[0]):
        out_ref[dest] = partial[0:8, :]


def image_kernel(
    coarse_ref, inv_ref, ids_ref, place_ref, arr_ref, pair_ref, dir_ref, res_ref, scale_ref,
    image_ref, sums_ref, mid_ref, prod_ref, high_ref, low_ref, piece_ref, table_ref,
):
    total = coarse_ref[0]
    for src in range(1, coarse_ref.shape[0]):
        total = total + coarse_ref[src]
    mid_ref[...] = total
    coarse_rows = [jnp.broadcast_to(mid_ref[q : q + 1, :], (LANES, LANES)) for q in range(8)]

    ids = ids_ref[...]
    ids_high = lax.shift_right_arithmetic(ids, 7)
    ids_low = jnp.bitwise_and(ids, LANES - 1)
    ones = jnp.ones((8, LANES), F32)
    lifted = jnp.zeros((8, LANES), F32)
    for block in range(8):
        rows = slice(block * LANES, (block + 1) * LANES)
        product = inv_ref[rows, 0:LANES] * coarse_rows[0]
        for q in range(1, 8):
            product = product + inv_ref[rows, q * LANES : (q + 1) * LANES] * coarse_rows[q]
        prod_ref[...] = product
        lifted_row = full_dot(ones, prod_ref[...], ((1,), (1,)))
        picked = jnp.take_along_axis(lifted_row, ids_low, axis=1, mode="promise_in_bounds")
        lifted = jnp.where(ids_high == block, picked, lifted)

    split_index(place_ref, high_ref, low_ref)
    for c, piece in enumerate(split_channels(lifted, 3)):
        piece_ref[c] = piece
    rows = table_ref.shape[0]
    table_ref[...] = arr_ref[...].reshape(rows, LANES) + scatter_rows(
        rows,
        lambda t, r: high_ref[pl.ds(r, 1), :],
        lambda t, r: low_ref[pl.ds(r, 1), :],
        lambda c, t, r: piece_ref[c, pl.ds(r, 1), :],
        8,
        8,
        3,
    )

    def table_row(a):
        row = (a // 4) * 8 + a % 4
        return table_ref[row : row + 1, :]

    half = dir_ref.shape[0]

    def block(t, sums):
        start = pl.multiple_of(t * 8, 8)
        both = jnp.concatenate(
            [pair_ref[pl.ds(start, 8), :], pair_ref[pl.ds(half + start, 8), :]], axis=0
        )
        picked = gather_block(both, table_row, rows // 2, 2)
        image = picked[0:8] - picked[8:16]
        image_ref[pl.ds(start, 8), :] = image
        res = res_ref[pl.ds(start, 8), :]
        scaled = scale_ref[pl.ds(start, 8), :]
        scaled_res = res * scaled
        return (
            sums[0] + scaled_res * res,
            sums[1] + dir_ref[pl.ds(start, 8), :] * image,
            sums[2] + scaled_res * image,
            sums[3] + (scaled * image) * image,
        )

    zero = jnp.zeros((8, LANES), F32)
    sums = lax.fori_loop(0, half // 8, block, (zero, zero, zero, zero))
    lane = lax.broadcasted_iota(jnp.int32, (8, LANES), 1)
    packed = jnp.zeros((8, LANES), F32)
    for n, part in enumerate(sums):
        value = jnp.sum(jnp.sum(part, axis=0, keepdims=True), axis=1, keepdims=True)
        packed = jnp.where(lane == n, jnp.broadcast_to(value, (8, LANES)), packed)
    for t in range(sums_ref.shape[0] // 8):
        sums_ref[8 * t : 8 * t + 8, :] = packed


def update_kernel(
    sums_ref, iterate_ref, res_ref, dir_ref, scale_ref, image_ref, it_out, res_out, dir_out
):
    totals = jnp.sum(sums_ref[...], axis=0, keepdims=True)
    lane = lax.broadcasted_iota(jnp.int32, (1, LANES), 1)

    def pick(n):
        return jnp.sum(jnp.where(lane == n, totals, 0.0), axis=1, keepdims=True)

    old, curvature, cross, square = pick(0), pick(1), pick(2), pick(3)
    alpha = old / curvature
    new = old - 2.0 * alpha * cross + (alpha * alpha) * square
    beta = new / old
    direction = dir_ref[...]
    res_next = res_ref[...] - alpha * image_ref[...]
    it_out[...] = iterate_ref[...] + alpha * direction
    res_out[...] = res_next
    dir_out[...] = scale_ref[...] * res_next + beta * direction


def slot_index(cells):
    plane = cells // 252
    spot = cells % 252
    slot = (
        spot
        + (spot >= 64).astype(jnp.int32)
        + 2 * (spot >= 126).astype(jnp.int32)
        + (spot >= 188).astype(jnp.int32)
    )
    along_x = plane // 12
    patch = (plane % 12) // 3
    component = plane % 3
    row = patch * 48 + (slot // LANES) * 24 + component * 8 + along_x
    return row * LANES + slot % LANES


def exchange(array, axis):
    return lax.all_to_all(array, axis, split_axis=0, concat_axis=0, tiled=True)


def solve_constants(basis, values, coeffs, pencil):
    patch, half = pencil // 2, pencil % 2
    own = lax.dynamic_index_in_dim(basis, patch, 0, keepdims=False)
    own_values = lax.dynamic_index_in_dim(values, patch, 0, keepdims=False)
    own_coeffs = lax.dynamic_index_in_dim(coeffs, patch, 0, keepdims=False)
    half_x = lax.dynamic_slice(own[0], (0, half * 32), (64, 32))
    rows = jnp.arange(192, dtype=jnp.int32)[:, None] // 64
    lanes = jnp.arange(LANES, dtype=jnp.int32)[None, :] // 32
    along_x = jnp.where(rows == lanes, jnp.tile(half_x, (3, 4)), 0.0)
    blocks = jnp.arange(256, dtype=jnp.int32) // 64
    stacked = jnp.tile(jnp.concatenate([own[2], own[1], own[1], own[2]], axis=0), (1, 4))
    block_basis = jnp.where(blocks[:, None] == blocks[None, :], stacked, 0.0)

    def spread(column):
        return jnp.broadcast_to(column[:, None], (64, LANES))

    lane = jnp.arange(LANES, dtype=jnp.int32)
    pad = lane >= 96
    weights = jnp.where(
        pad[:, None], 0.0, jnp.concatenate([jnp.repeat(own_coeffs, 32, axis=0), own_coeffs[:1].repeat(32, axis=0)], axis=0)
    )
    half_values = lax.dynamic_slice(own_values[0], (half * 32,), (32,))
    x_term = jnp.where(pad, 1.0, weights[:, 0] * jnp.tile(half_values, 4))
    xy_term = x_term[None, :] + weights[None, :, 1] * own_values[1][:, None]
    z_term = weights[None, :, 2] * own_values[2][:, None]
    constants = jnp.stack(
        [
            spread(own[1][0]),
            spread(own[1][63]),
            spread(own[2][0]),
            spread(own[2][63]),
            xy_term,
            z_term,
        ]
    )
    return along_x.T, along_x, block_basis.T, block_basis, constants


def body(
    mult_iterate,
    residual,
    direction,
    mult_scale,
    eigen_basis,
    eigen_values,
    elastic_coef,
    coarse_inverse,
    send_pos,
    pair_slots,
    prim_rows,
    coarse_idx,
):
    group = lax.axis_index("group")
    pencil = lax.axis_index("pencil")
    groups = lax.axis_size("group")
    pencils = lax.axis_size("pencil")
    iterate_now = mult_iterate.reshape(64, LANES)
    resid_now = residual.reshape(64, LANES)
    search_dir = direction.reshape(64, LANES)
    scale_now = mult_scale.reshape(64, LANES)
    pair_rows = pair_slots.reshape(128, LANES)
    slots = slot_index(send_pos.reshape(128, LANES))
    primal = prim_rows[0, 0]
    coarse_ids = coarse_idx[0, 0]

    lane_group = jnp.arange(LANES, dtype=jnp.int32) // 32
    mine = lane_group == group % 4
    extra = jnp.zeros((8, LANES), F32)
    extra = extra.at[0].set(jnp.where(mine, jnp.tile(primal, 4), 0).astype(F32))
    extra = extra.at[1].set(jnp.where(mine, jnp.tile(coarse_ids, 4), 0).astype(F32))

    index_scratch = [pltpu.VMEM((128, LANES), F32), pltpu.VMEM((128, LANES), F32)]
    back = call(
        back_kernel,
        jax.ShapeDtypeStruct((groups, 8, LANES), F32),
        3,
        "back",
        index_scratch + [pltpu.VMEM((2, 128, LANES), F32), pltpu.VMEM((128, LANES), F32)],
    )(pair_rows, search_dir, extra)
    arrived = exchange(back, "group")

    loads = call(
        load_kernel,
        jax.ShapeDtypeStruct((pencils, 24, 256), F32),
        2,
        "load",
        index_scratch + [pltpu.VMEM((2, 256, LANES), F32), pltpu.VMEM((192, LANES), F32)],
    )(arrived, slots)
    columns = exchange(loads, "pencil")

    constants = solve_constants(eigen_basis, eigen_values, elastic_coef, pencil)
    partial = call(
        solve_kernel,
        jax.ShapeDtypeStruct((pencils, 24, 256), F32),
        6,
        "solve",
        [
            pltpu.VMEM((256, LANES), F32),
            pltpu.VMEM((64, 8, LANES), F32),
            pltpu.VMEM((64, 8, LANES), F32),
        ],
    )(columns, *constants)
    slabs = exchange(partial, "pencil")

    primal_slots = slots.reshape(-1)[primal]
    extra_slots = jnp.full((16, LANES), -1, jnp.int32)
    extra_slots = extra_slots.at[0].set(jnp.where(mine, jnp.tile(primal_slots, 4), -1))
    picked = call(
        pick_kernel,
        jax.ShapeDtypeStruct((groups, 8, LANES), F32),
        2,
        "pick",
        [pltpu.VMEM((192, LANES), F32), pltpu.VMEM((144, LANES), F32)],
    )(slabs, jnp.concatenate([slots, extra_slots], axis=0))
    owner = exchange(picked, "group")

    packed = jnp.sum(arrived[:, 4:6, :].reshape(8, 4, 2, LANES), axis=1).astype(jnp.int32)
    their_primal = packed[:, 0]
    their_ids = packed[:, 1]
    sender = 4 * jnp.arange(8, dtype=jnp.int32)[:, None] + lane_group[None, :]
    local = their_primal - group * 512
    valid = (local >= 0) & (local < 512)
    place = jnp.where(valid, (sender * 8 + local // LANES) * LANES + local % LANES, -1)

    small_index = [pltpu.VMEM((8, LANES), F32), pltpu.VMEM((8, LANES), F32)]
    coarse_part = call(
        coarse_kernel,
        jax.ShapeDtypeStruct((pencils, 8, LANES), F32),
        2,
        "coarse",
        small_index + [pltpu.VMEM((3, 8, LANES), F32)],
    )(owner, their_ids)
    coarse_all = exchange(coarse_part, "pencil")

    image, sums = call(
        image_kernel,
        (
            jax.ShapeDtypeStruct((64, LANES), F32),
            jax.ShapeDtypeStruct((groups * pencils, LANES), F32),
        ),
        9,
        "image",
        [pltpu.VMEM((8, LANES), F32), pltpu.VMEM((LANES, LANES), F32)]
        + small_index
        + [pltpu.VMEM((3, 8, LANES), F32), pltpu.VMEM((256, LANES), F32)],
    )(
        coarse_all, coarse_inverse, their_ids, place, owner, pair_rows, search_dir, resid_now,
        scale_now,
    )
    totals = exchange(sums, ("group", "pencil"))

    shape = jax.ShapeDtypeStruct((64, LANES), F32)
    outs = call(update_kernel, (shape, shape, shape), 6, "update")(
        totals, iterate_now, resid_now, search_dir, scale_now, image
    )
    return tuple(out.reshape(1, 1, -1) for out in outs)


def solution(mesh):
    in_specs = (
        P("group", "pencil", None),
        P("group", "pencil", None),
        P("group", "pencil", None),
        P("group", "pencil", None),
        P("group", None, None, None),
        P("group", None, None),
        P("group", None, None),
        P(),
        P("group", "pencil", None),
        P("group", "pencil", None, None),
        P("group", "pencil", None),
        P("group", "pencil", None),
    )
    out_specs = (P("group", "pencil", None), P("group", "pencil", None), P("group", "pencil", None))
    return jax.shard_map(body, mesh=mesh, in_specs=in_specs, out_specs=out_specs, check_vma=False)
```

```python
import jax
import jax.numpy as jnp
from jax import lax
from jax.experimental import pallas as pl
from jax.experimental.pallas import tpu as pltpu
from jax.sharding import PartitionSpec as P

LANES = 128
BF16 = jnp.bfloat16
F32 = jnp.float32
HIGHEST = lax.Precision.HIGHEST
VMEM = pl.BlockSpec(memory_space=pltpu.VMEM)


HBM = pl.BlockSpec(memory_space=pltpu.HBM)


def call(kernel, out_shape, in_specs, name, scratch=(), flops=4_000_000):
    single = not isinstance(out_shape, (tuple, list))
    return pl.pallas_call(
        kernel,
        out_shape=out_shape,
        in_specs=in_specs,
        out_specs=VMEM if single else [VMEM] * len(out_shape),
        scratch_shapes=list(scratch),
        name=name,
        compiler_params=pltpu.CompilerParams(vmem_limit_bytes=16 << 20),
        cost_estimate=pl.CostEstimate(flops=flops, bytes_accessed=1 << 18, transcendentals=0),
    )


def split_channels(value, count):
    pieces = []
    for _ in range(count):
        piece = value.astype(BF16).astype(F32)
        pieces.append(piece)
        value = value - piece
    return pieces


def one_hot_parts(rows, high_row, low_row, piece_rows, chunk, channels):
    row_ids = lax.broadcasted_iota(jnp.int32, (rows, LANES), 0).astype(F32).astype(BF16)
    lane_ids = lax.broadcasted_iota(jnp.int32, (LANES, LANES), 0).astype(F32).astype(BF16)
    left, right = [], []
    for r in range(chunk):
        high = jnp.broadcast_to(high_row(r), (rows, LANES)).astype(BF16)
        low = jnp.broadcast_to(low_row(r), (LANES, LANES)).astype(BF16)
        left.append(jnp.where(row_ids == high, BF16(1), BF16(0)))
        match = lane_ids == low
        pieces = [
            jnp.where(
                match, jnp.broadcast_to(piece_rows(n, r), (LANES, LANES)).astype(BF16), BF16(0)
            )
            for n in range(channels)
        ]
        right.append(jnp.concatenate(pieces, axis=0))
    return jnp.concatenate(left, axis=1), jnp.concatenate(right, axis=1)


def pair_dot(left, right):
    return lax.dot_general(left, right, (((1,), (1,)), ((), ())), preferred_element_type=F32)


def scatter_large(rows, high_ref, low_ref, piece_row, total, chunk):
    def step(index, acc):
        left, right = one_hot_parts(
            rows,
            lambda r: high_ref[pl.ds(index * chunk + r, 1), :],
            lambda r: low_ref[pl.ds(index * chunk + r, 1), :],
            lambda n, r: piece_row(n, index, r),
            chunk,
            2,
        )
        return acc + pair_dot(right, left)

    acc = lax.fori_loop(0, total // chunk, step, jnp.zeros((2 * LANES, rows), F32))
    return (acc[:LANES] + acc[LANES:]).T


def scatter_small(rows, high_ref, low_ref, piece_ref, count):
    left, right = one_hot_parts(
        rows,
        lambda r: high_ref[r : r + 1, :],
        lambda r: low_ref[r : r + 1, :],
        lambda n, r: piece_ref[n, r : r + 1, :],
        count,
        3,
    )
    acc = pair_dot(left, right)
    return acc[:, :LANES] + acc[:, LANES : 2 * LANES] + acc[:, 2 * LANES :]


def gather_rows(indices, table_row, table_rows):
    high = lax.shift_right_arithmetic(indices, 7)
    low = jnp.bitwise_and(indices, LANES - 1)
    acc = [jnp.zeros(indices.shape, F32) for _ in range(2)]
    for a in range(table_rows):
        row = jnp.broadcast_to(table_row(a), indices.shape)
        picked = jnp.take_along_axis(row, low, axis=1, mode="promise_in_bounds")
        acc[a % 2] = jnp.where(high == a, picked, acc[a % 2])
    return acc[0] + acc[1]


def store_digits(idx, high_ref, low_ref):
    high_ref[...] = lax.shift_right_arithmetic(idx, 7).astype(F32)
    low_ref[...] = jnp.bitwise_and(idx, LANES - 1).astype(F32)


def floor_div(value, divisor):
    return jnp.floor((value + 0.5) * (1.0 / divisor))


def cell_digits(cells):
    cells = cells.astype(F32)
    plane = floor_div(cells, 252)
    spot = cells - 252.0 * plane
    slot = (
        spot
        + jnp.where(spot >= 64.0, 1.0, 0.0)
        + jnp.where(spot >= 126.0, 2.0, 0.0)
        + jnp.where(spot >= 188.0, 1.0, 0.0)
    )
    along_x = floor_div(plane, 12)
    rest = plane - 12.0 * along_x
    patch = floor_div(rest, 3)
    component = rest - 3.0 * patch
    half = jnp.where(slot >= 128.0, 1.0, 0.0)
    return patch, component, along_x, half, slot - 128.0 * half


def own_lanes():
    lane = lax.broadcasted_iota(jnp.int32, (1, LANES), 1)
    return lax.shift_right_logical(lane, 5)


def spread_lanes(row):
    return jnp.concatenate([row] * 4, axis=1)


CHUNK = 32
OWNER_ROWS = 14


def start_copies(pairs, sems):
    copies = [
        pltpu.make_async_copy(source, target, sems.at[n])
        for n, (source, target) in enumerate(pairs)
    ]
    for copy in copies:
        copy.start()
    return copies


def back_kernel(
    pair_hbm, dir_hbm, cells_hbm, prim_hbm, ids_hbm, basis_hbm, values_hbm, coeff_hbm,
    out_ref, idx_ref, cells_ref, small_ref, bxt_ref, bx_ref, bdt_ref, bd_ref, cst_ref,
    pair_ref, dir_ref, prim_ref, ids_ref, basis_ref, values_ref, coeff_ref,
    high_ref, low_ref, piece_ref, sems,
):
    pencil = lax.axis_index("pencil")
    patch = lax.div(pencil, 2)
    side = lax.rem(pencil, 2)
    copies = start_copies(
        [
            (pair_hbm, pair_ref),
            (dir_hbm, dir_ref),
            (cells_hbm, cells_ref),
            (prim_hbm, prim_ref),
            (ids_hbm, ids_ref),
            (basis_hbm.at[patch], basis_ref),
            (values_hbm, values_ref),
            (coeff_hbm, coeff_ref),
        ],
        sems,
    )
    half = dir_ref.shape[0]
    bx_ref[...] = jnp.zeros(bx_ref.shape, F32)
    bxt_ref[...] = jnp.zeros(bxt_ref.shape, F32)
    bd_ref[...] = jnp.zeros(bd_ref.shape, F32)
    bdt_ref[...] = jnp.zeros(bdt_ref.shape, F32)
    copies[0].wait()
    copies[1].wait()
    for k in range(half):
        both = pair_ref[:, k * LANES : (k + 1) * LANES]
        idx_ref[k : k + 1, :] = both[0:1]
        idx_ref[half + k : half + k + 1, :] = both[1:2]
    store_digits(idx_ref[...], high_ref, low_ref)
    for n, piece in enumerate(split_channels(dir_ref[...], 2)):
        piece_ref[n, :half, :] = piece
        piece_ref[n, half:, :] = -piece
    out_ref[...] = scatter_large(
        2 * half,
        high_ref,
        low_ref,
        lambda n, t, r: piece_ref[n, pl.ds(t * CHUNK + r, 1), :],
        2 * half,
        CHUNK,
    )
    for copy in copies[2:]:
        copy.wait()
    small_ref[...] = jnp.zeros(small_ref.shape, F32)
    small_ref[0:1, :] = spread_lanes(prim_ref[...].astype(F32))
    small_ref[1:2, :] = spread_lanes(ids_ref[...].astype(F32))
    along_x, along_y, along_z = basis_ref[0], basis_ref[1], basis_ref[2]
    first = lax.broadcasted_iota(jnp.int32, (64, 64), 0)
    second = lax.broadcasted_iota(jnp.int32, (64, 64), 1)
    identity = jnp.where(first == second, 1.0, 0.0)
    half_x = jnp.where(side == 1, along_x[:, 32:64], along_x[:, 0:32])
    flipped = full_dot(identity, along_x, ((1,), (1,)))
    half_flipped = jnp.where(side == 1, flipped[32:64], flipped[0:32])
    for c in range(3):
        bx_ref[64 * c : 64 * c + 64, 32 * c : 32 * c + 32] = half_x
        bxt_ref[32 * c : 32 * c + 32, 64 * c : 64 * c + 64] = half_flipped
    flipped_y = full_dot(identity, along_y, ((1,), (1,)))
    flipped_z = full_dot(identity, along_z, ((1,), (1,)))
    for block in range(4):
        part = slice(64 * block, 64 * block + 64)
        bd_ref[part, part] = along_z if block in (0, 3) else along_y
        bdt_ref[part, part] = flipped_z if block in (0, 3) else flipped_y

    def spread(column):
        return jnp.broadcast_to(column, (64, LANES))

    cst_ref[0] = spread(column_of(along_y[0:1]))
    cst_ref[1] = spread(column_of(along_y[63:64]))
    cst_ref[2] = spread(column_of(along_z[0:1]))
    cst_ref[3] = spread(column_of(along_z[63:64]))
    lane = lax.broadcasted_iota(jnp.int32, (1, LANES), 1)

    def weight(dim):
        value = jnp.zeros((1, LANES), F32)
        for c in range(3):
            here = lax.shift_right_logical(lane, 5) == c
            coeff = coeff_ref[c, pl.ds(patch, 1), :][:, dim : dim + 1]
            value = jnp.where(here, jnp.broadcast_to(coeff, (1, LANES)), value)
        return value

    x_values, y_values, z_values = (values_ref[dim, pl.ds(patch, 1), :] for dim in range(3))
    half_values = jnp.where(side == 1, x_values[:, 32:64], x_values[:, 0:32])
    x_term = jnp.where(lane >= 96, 1.0, weight(0) * spread_lanes(half_values))
    y_term = weight(1) * spread(column_of(y_values))
    cst_ref[4] = x_term + y_term
    cst_ref[5] = weight(2) * spread(column_of(z_values))


def load_kernel(
    arr_ref, pos_ref, small_ref, out_ref, slots_ref, high_ref, low_ref, piece_ref, acc_ref
):
    patch, component, along_x, half, lane = cell_digits(pos_ref[...])
    row = patch * 48.0 + half * 24.0 + component * 8.0 + along_x
    high_ref[...] = row
    low_ref[...] = lane
    slots_ref[...] = (row * 128.0 + lane).astype(jnp.int32)
    rows = pos_ref.shape[0]
    for n, piece in enumerate(split_channels(arr_ref[...], 2)):
        piece_ref[n] = piece
    acc_ref[...] = scatter_large(
        acc_ref.shape[0],
        high_ref,
        low_ref,
        lambda n, t, r: piece_ref[n, pl.ds(t * CHUNK + r, 1), :],
        rows,
        CHUNK,
    )
    pencil = lax.axis_index("pencil")
    mine = own_lanes() == lax.rem(pencil, 4)
    primal = jnp.broadcast_to(small_ref[0:1, :], (8, LANES)).astype(jnp.int32)
    cells = gather_rows(primal, lambda a: pos_ref[a : a + 1, :].astype(F32), rows)
    patch, component, along_x, half, lane = cell_digits(cells[0:1])
    place = half * 192.0 + component * 64.0 + along_x + (8 * pencil).astype(F32)
    code = place * 128.0 + lane
    ids = jnp.where(mine, small_ref[1:2, :], 0.0)
    for dest in range(out_ref.shape[0]):
        for side in range(2):
            start = (dest // 2) * 48 + side * 24
            out_ref[dest, 0:24, side * LANES : (side + 1) * LANES] = acc_ref[start : start + 24, :]
        own = jnp.where(patch == float(dest // 2), code, -1.0)
        out_ref[dest, 24:32, :] = jnp.zeros((8, 256), F32)
        out_ref[dest, 24:25, 0:LANES] = jnp.where(mine, own, 0.0)
        out_ref[dest, 24:25, LANES:] = ids


def full_dot(left, right, contract):
    return lax.dot_general(
        left, right, ((contract[0], contract[1]), ((), ())), precision=HIGHEST,
        preferred_element_type=F32,
    )


def column_of(row):
    count = row.shape[1]
    first = lax.broadcasted_iota(jnp.int32, (count, count), 0)
    second = lax.broadcasted_iota(jnp.int32, (count, count), 1)
    spread = jnp.broadcast_to(row, (count, count))
    return jnp.sum(jnp.where(first == second, spread, 0.0), axis=1, keepdims=True)


def solve_kernel(
    recv_ref, bxt_ref, bx_ref, bdt_ref, bd_ref, cst_ref, out_ref, fwd_ref, d0_ref, d1_ref,
    slab_ref, high_ref, low_ref, piece_ref,
):
    sources = recv_ref.shape[0]
    load = jnp.concatenate(
        [recv_ref[src, 8 * c : 8 * c + 8, :] for c in range(3) for src in range(sources)], axis=0
    )
    along_x = full_dot(bxt_ref[...], load, ((1,), (0,)))
    fwd_ref[...] = full_dot(bdt_ref[...], along_x, ((1,), (1,)))

    def step(j, carry):
        top, bottom = carry

        def row(index):
            return jnp.broadcast_to(cst_ref[index, pl.ds(j, 1), :], (64, LANES))

        first = jnp.broadcast_to(fwd_ref[pl.ds(64 + j, 1), :], (64, LANES))
        last = jnp.broadcast_to(fwd_ref[pl.ds(128 + j, 1), :], (64, LANES))
        y_first, y_last = row(0), row(1)
        spectral = (
            y_first * fwd_ref[0:64, :]
            + y_last * fwd_ref[192:256, :]
            + first * cst_ref[2]
            + last * cst_ref[3]
        )
        scaled = spectral / (row(4) + cst_ref[5])
        along_first = cst_ref[2] * scaled
        along_last = cst_ref[3] * scaled
        d0_ref[j] = jnp.sum(along_first.reshape(8, 8, LANES), axis=0)
        d1_ref[j] = jnp.sum(along_last.reshape(8, 8, LANES), axis=0)
        return top + y_first * scaled, bottom + y_last * scaled

    zero = jnp.zeros((64, LANES), F32)
    top, bottom = lax.fori_loop(0, 64, step, (zero, zero), unroll=4)
    edges = jnp.concatenate(
        [top, jnp.sum(d0_ref[...], axis=1), jnp.sum(d1_ref[...], axis=1), bottom], axis=0
    )
    cells = full_dot(bd_ref[...], edges, ((1,), (0,)))
    slab_ref[...] = full_dot(bx_ref[...], cells, ((1,), (1,)))

    def packed(lanes):
        halves = []
        for part in range(2):
            row = recv_ref[4 * part, 24:25, lanes]
            for k in range(1, 4):
                row = row + recv_ref[4 * part + k, 24:25, lanes]
            halves.append(row)
        return jnp.concatenate(halves + [jnp.full((6, LANES), -1.0, F32)], axis=0)

    codes = packed(slice(0, LANES)).astype(jnp.int32)
    ids = packed(slice(LANES, 256)).astype(jnp.int32)
    primal = gather_rows(
        codes,
        lambda a: slab_ref[a % 192 : a % 192 + 1, (a // 192) * LANES : (a // 192 + 1) * LANES],
        384,
    )
    store_digits(ids, high_ref, low_ref)
    for n, piece in enumerate(split_channels(primal, 3)):
        piece_ref[n] = piece
    partial = scatter_small(16, high_ref, low_ref, piece_ref, 2)
    for dest in range(out_ref.shape[0]):
        for c in range(3):
            start = 64 * c + 8 * dest
            out_ref[dest, 8 * c : 8 * c + 8, :] = slab_ref[start : start + 8, :]
        out_ref[dest, 24:32, 0:LANES] = partial[0:8, :]
        out_ref[dest, 24:32, LANES:] = jnp.zeros((8, LANES), F32)


def pick_kernel(
    recv_ref, idx_ref, small_ref, inv_hbm, out_ref, table_ref, pick_ref, inv_ref, mid_ref, prod_ref,
    lift_ref, sem,
):
    copy = pltpu.make_async_copy(inv_hbm, inv_ref, sem)
    copy.start()
    coarse = recv_ref[0, 24:32, 0:LANES]
    for src in range(1, recv_ref.shape[0]):
        coarse = coarse + recv_ref[src, 24:32, 0:LANES]
    for p in range(recv_ref.shape[0] // 2):
        for half in range(2):
            lanes = slice(half * LANES, (half + 1) * LANES)
            start = p * 48 + half * 24
            table_ref[start : start + 24, :] = (
                recv_ref[2 * p, 0:24, lanes] + recv_ref[2 * p + 1, 0:24, lanes]
            )
    table_rows = table_ref.shape[0]

    def block(t, carry):
        for sub in range(4):
            start = pl.multiple_of(t * 32 + sub * 8, 8)
            pick_ref[pl.ds(start, 8), :] = gather_rows(
                idx_ref[pl.ds(start, 8), :], lambda a: table_ref[a : a + 1, :], table_rows
            )
        return carry

    lax.fori_loop(0, 4, block, 0)
    mid_ref[...] = coarse
    copy.wait()
    coarse_rows = [jnp.broadcast_to(mid_ref[q : q + 1, :], (LANES, LANES)) for q in range(8)]
    ones = jnp.ones((8, LANES), F32)
    for part in range(8):
        rows = slice(part * LANES, (part + 1) * LANES)
        product = inv_ref[rows, 0:LANES] * coarse_rows[0]
        for q in range(1, 8):
            product = product + inv_ref[rows, q * LANES : (q + 1) * LANES] * coarse_rows[q]
        prod_ref[part] = product
        lift_ref[part : part + 1, :] = full_dot(ones, prod_ref[part], ((1,), (1,)))[0:1]
    lift = lift_ref[...]
    mine = own_lanes() == lax.rem(lax.axis_index("group"), 4)
    extra = jnp.where(mine, small_ref[0:2, :], 0.0)
    for h in range(pick_ref.shape[0] // 4):
        start = OWNER_ROWS * h
        out_ref[start : start + 8, :] = lift
        out_ref[start + 8 : start + 12, :] = pick_ref[4 * h : 4 * h + 4, :]
        out_ref[start + 12 : start + 14, :] = extra


def image_kernel(
    own_ref, pair_ref, dir_hbm, res_hbm, scale_hbm, iterate_hbm,
    image_ref, sums_ref, dir_ref, res_ref, scale_ref, iterate_ref,
    lift_ref, high_ref, low_ref, piece_ref, corr_ref, table_ref, sems,
):
    copies = start_copies(
        [
            (dir_hbm, dir_ref),
            (res_hbm, res_ref),
            (scale_hbm, scale_ref),
            (iterate_hbm, iterate_ref),
        ],
        sems,
    )
    groups = own_ref.shape[0] // OWNER_ROWS
    total = own_ref[0:8, :]
    for h in range(1, groups):
        total = total + own_ref[OWNER_ROWS * h : OWNER_ROWS * h + 8, :]
    lift_ref[...] = total

    def packed(row):
        rows = []
        for q in range(8):
            start = OWNER_ROWS * 4 * q + row
            value = own_ref[start : start + 1, :]
            for k in range(1, 4):
                start = OWNER_ROWS * (4 * q + k) + row
                value = value + own_ref[start : start + 1, :]
            rows.append(value)
        return jnp.concatenate(rows, axis=0).astype(jnp.int32)

    local = packed(12) - 512 * lax.axis_index("group")
    ids = packed(13)
    sender = 4 * lax.broadcasted_iota(jnp.int32, (8, LANES), 0) + jnp.broadcast_to(
        own_lanes(), (8, LANES)
    )
    valid = jnp.logical_and(local >= 0, local < 512)
    store_digits(jnp.where(valid, sender * 512 + local, -1), high_ref, low_ref)

    lifted = gather_rows(ids, lambda a: lift_ref[a : a + 1, :], 8)
    for n, piece in enumerate(split_channels(lifted, 3)):
        piece_ref[n] = piece
    corr_ref[...] = scatter_small(4 * groups, high_ref, low_ref, piece_ref, 8)
    for h in range(groups):
        start = OWNER_ROWS * h + 8
        table_ref[4 * h : 4 * h + 4, :] = (
            own_ref[start : start + 4, :] + corr_ref[4 * h : 4 * h + 4, :]
        )
    for copy in copies:
        copy.wait()

    half = dir_ref.shape[0]
    table_rows = 4 * groups

    def block(t, sums):
        sums = list(sums)
        for sub in range(2):
            start = pl.multiple_of(t * 16 + sub * 8, 8)
            plus, minus = (
                gather_rows(
                    pair_ref[pl.ds(base + start, 8), :],
                    lambda a: table_ref[a : a + 1, :],
                    table_rows,
                )
                for base in (0, half)
            )
            image = plus - minus
            image_ref[pl.ds(start, 8), :] = image
            res = res_ref[pl.ds(start, 8), :]
            scaled = scale_ref[pl.ds(start, 8), :]
            scaled_res = res * scaled
            sums[0] = sums[0] + scaled_res * res
            sums[1] = sums[1] + dir_ref[pl.ds(start, 8), :] * image
            sums[2] = sums[2] + scaled_res * image
            sums[3] = sums[3] + (scaled * image) * image
        return tuple(sums)

    zero = jnp.zeros((8, LANES), F32)
    sums = lax.fori_loop(0, half // 16, block, (zero, zero, zero, zero))
    lane = lax.broadcasted_iota(jnp.int32, (8, LANES), 1)
    packed_sums = jnp.zeros((8, LANES), F32)
    for n, part in enumerate(sums):
        value = jnp.sum(jnp.sum(part, axis=0, keepdims=True), axis=1, keepdims=True)
        packed_sums = jnp.where(lane == n, jnp.broadcast_to(value, (8, LANES)), packed_sums)
    for t in range(sums_ref.shape[0] // 8):
        sums_ref[8 * t : 8 * t + 8, :] = packed_sums


def update_kernel(
    sums_ref, dir_ref, res_ref, scale_ref, iterate_ref, image_ref, it_out, res_out, dir_out
):
    totals = jnp.sum(sums_ref[...], axis=0, keepdims=True)
    lane = lax.broadcasted_iota(jnp.int32, (1, LANES), 1)

    def pick(n):
        return jnp.sum(jnp.where(lane == n, totals, 0.0), axis=1, keepdims=True)

    old, curvature, cross, square = pick(0), pick(1), pick(2), pick(3)
    alpha = old / curvature
    new = old - 2.0 * alpha * cross + (alpha * alpha) * square
    beta = new / old
    direction = dir_ref[...]
    res_next = res_ref[...] - alpha * image_ref[...]
    it_out[...] = iterate_ref[...] + alpha * direction
    res_out[...] = res_next
    dir_out[...] = scale_ref[...] * res_next + beta * direction


def exchange(array, axis):
    return lax.all_to_all(array, axis, split_axis=0, concat_axis=0, tiled=True)


def f32(*shape):
    return jax.ShapeDtypeStruct(shape, F32)


def i32(*shape):
    return jax.ShapeDtypeStruct(shape, jnp.int32)


def body(
    mult_iterate,
    residual,
    direction,
    mult_scale,
    eigen_basis,
    eigen_values,
    elastic_coef,
    coarse_inverse,
    send_pos,
    pair_slots,
    prim_rows,
    coarse_idx,
):
    groups = lax.axis_size("group")
    pencils = lax.axis_size("pencil")
    iterate_now = mult_iterate.reshape(64, LANES)
    resid_now = residual.reshape(64, LANES)
    search_dir = direction.reshape(64, LANES)
    scale_now = mult_scale.reshape(64, LANES)
    cells = send_pos.reshape(128, LANES)
    pairs = pair_slots.reshape(2, 8192)
    primal = prim_rows.reshape(1, 32)
    coarse_ids = coarse_idx.reshape(1, 32)

    def resident(array):
        return pltpu.with_memory_space_constraint(array, pltpu.HBM)

    digits = [pltpu.VMEM((128, LANES), F32), pltpu.VMEM((128, LANES), F32)]
    pieces = pltpu.VMEM((2, 128, LANES), F32)
    small = [
        pltpu.VMEM((8, LANES), F32),
        pltpu.VMEM((8, LANES), F32),
        pltpu.VMEM((3, 8, LANES), F32),
    ]
    sources = (
        pairs,
        search_dir,
        cells,
        primal,
        coarse_ids,
        eigen_basis,
        eigen_values.transpose(1, 0, 2),
        elastic_coef.transpose(1, 0, 2),
    )
    back, pair_rows, cells, primals, *constants = call(
        back_kernel,
        (
            f32(128, LANES),
            i32(128, LANES),
            i32(128, LANES),
            f32(8, LANES),
            f32(128, 192),
            f32(192, 128),
            f32(256, 256),
            f32(256, 256),
            f32(6, 64, LANES),
        ),
        [HBM] * len(sources),
        "back",
        [
            pltpu.VMEM((2, 8192), jnp.int32),
            pltpu.VMEM((64, LANES), F32),
            pltpu.VMEM((1, 32), jnp.int32),
            pltpu.VMEM((1, 32), jnp.int32),
            pltpu.VMEM((3, 64, 64), F32),
            pltpu.VMEM((3, 4, 64), F32),
            pltpu.VMEM((3, 4, 3), F32),
        ]
        + digits
        + [pieces, pltpu.SemaphoreType.DMA((len(sources),))],
    )(*(resident(source) for source in sources))
    arrived = exchange(back.reshape(groups, 4, LANES), "group").reshape(128, LANES)

    loads, slots = call(
        load_kernel,
        (f32(pencils, 32, 256), i32(128, LANES)),
        [VMEM] * 3,
        "load",
        digits + [pieces, pltpu.VMEM((192, LANES), F32)],
    )(arrived, cells, primals)
    columns = exchange(loads, "pencil")

    partial = call(
        solve_kernel,
        f32(pencils, 32, 256),
        [VMEM] * 6,
        "solve",
        [
            pltpu.VMEM((256, LANES), F32),
            pltpu.VMEM((64, 8, LANES), F32),
            pltpu.VMEM((64, 8, LANES), F32),
            pltpu.VMEM((192, 256), F32),
        ]
        + small,
    )(columns, *constants)
    slabs = exchange(partial, "pencil")

    picked = call(
        pick_kernel,
        f32(groups * OWNER_ROWS, LANES),
        [VMEM, VMEM, VMEM, HBM],
        "pick",
        [
            pltpu.VMEM((192, LANES), F32),
            pltpu.VMEM((128, LANES), F32),
            pltpu.VMEM((1024, 1024), F32),
            pltpu.VMEM((8, LANES), F32),
            pltpu.VMEM((8, LANES, LANES), F32),
            pltpu.VMEM((8, LANES), F32),
            pltpu.SemaphoreType.DMA,
        ],
    )(slabs, slots, primals, resident(coarse_inverse))
    owner = exchange(picked.reshape(groups, 1, OWNER_ROWS * LANES), "group")

    shape = f32(64, LANES)
    image, sums, *vectors = call(
        image_kernel,
        (shape, f32(groups * pencils, LANES), shape, shape, shape, shape),
        [VMEM, VMEM] + [HBM] * 4,
        "image",
        [pltpu.VMEM((8, LANES), F32)]
        + small
        + [
            pltpu.VMEM((128, LANES), F32),
            pltpu.VMEM((128, LANES), F32),
            pltpu.SemaphoreType.DMA((4,)),
        ],
    )(
        owner.reshape(groups * OWNER_ROWS, LANES),
        pair_rows,
        *(resident(array) for array in (search_dir, resid_now, scale_now, iterate_now)),
    )
    totals = exchange(sums, ("group", "pencil"))

    outs = call(update_kernel, (shape, shape, shape), [VMEM] * 6, "update")(
        totals, *vectors, image
    )
    return tuple(out.reshape(1, 1, -1) for out in outs)


def solution(mesh):
    in_specs = (
        P("group", "pencil", None),
        P("group", "pencil", None),
        P("group", "pencil", None),
        P("group", "pencil", None),
        P("group", None, None, None),
        P("group", None, None),
        P("group", None, None),
        P(),
        P("group", "pencil", None),
        P("group", "pencil", None, None),
        P("group", "pencil", None),
        P("group", "pencil", None),
    )
    out_specs = (P("group", "pencil", None), P("group", "pencil", None), P("group", "pencil", None))
    return jax.shard_map(body, mesh=mesh, in_specs=in_specs, out_specs=out_specs, check_vma=False)
```

```python
import jax
import jax.numpy as jnp
from jax import lax
from jax.experimental import pallas as pl
from jax.experimental.pallas import tpu as pltpu
from jax.sharding import PartitionSpec as P

LANES = 128
BF16 = jnp.bfloat16
F32 = jnp.float32
HIGHEST = lax.Precision.HIGHEST
VMEM = pl.BlockSpec(memory_space=pltpu.VMEM)


HBM = pl.BlockSpec(memory_space=pltpu.HBM)


def call(kernel, out_shape, in_specs, name, scratch=(), flops=4_000_000):
    single = not isinstance(out_shape, (tuple, list))
    return pl.pallas_call(
        kernel,
        out_shape=out_shape,
        in_specs=in_specs,
        out_specs=VMEM if single else [VMEM] * len(out_shape),
        scratch_shapes=list(scratch),
        name=name,
        compiler_params=pltpu.CompilerParams(vmem_limit_bytes=16 << 20),
        cost_estimate=pl.CostEstimate(flops=flops, bytes_accessed=1 << 18, transcendentals=0),
    )


def split_channels(value, count):
    pieces = []
    for _ in range(count):
        piece = value.astype(BF16).astype(F32)
        pieces.append(piece)
        value = value - piece
    return pieces


def one_hot_parts(rows, high_row, low_row, piece_rows, chunk, channels):
    row_ids = lax.broadcasted_iota(jnp.int32, (rows, LANES), 0).astype(F32).astype(BF16)
    lane_ids = lax.broadcasted_iota(jnp.int32, (LANES, LANES), 0).astype(F32).astype(BF16)
    left, right = [], []
    for r in range(chunk):
        high = jnp.broadcast_to(high_row(r), (rows, LANES)).astype(BF16)
        low = jnp.broadcast_to(low_row(r), (LANES, LANES)).astype(BF16)
        left.append(jnp.where(row_ids == high, BF16(1), BF16(0)))
        match = lane_ids == low
        pieces = [
            jnp.where(
                match, jnp.broadcast_to(piece_rows(n, r), (LANES, LANES)).astype(BF16), BF16(0)
            )
            for n in range(channels)
        ]
        right.append(jnp.concatenate(pieces, axis=0))
    return jnp.concatenate(left, axis=1), jnp.concatenate(right, axis=1)


def pair_dot(left, right):
    return lax.dot_general(left, right, (((1,), (1,)), ((), ())), preferred_element_type=F32)


def scatter_large(rows, high_ref, low_ref, piece_row, total, chunk):
    def step(index, acc):
        left, right = one_hot_parts(
            rows,
            lambda r: high_ref[pl.ds(index * chunk + r, 1), :],
            lambda r: low_ref[pl.ds(index * chunk + r, 1), :],
            lambda n, r: piece_row(n, index, r),
            chunk,
            2,
        )
        return acc + pair_dot(right, left)

    acc = lax.fori_loop(0, total // chunk, step, jnp.zeros((2 * LANES, rows), F32))
    return (acc[:LANES] + acc[LANES:]).T


def scatter_small(rows, high_ref, low_ref, piece_ref, count):
    left, right = one_hot_parts(
        rows,
        lambda r: high_ref[r : r + 1, :],
        lambda r: low_ref[r : r + 1, :],
        lambda n, r: piece_ref[n, r : r + 1, :],
        count,
        3,
    )
    acc = pair_dot(left, right)
    return acc[:, :LANES] + acc[:, LANES : 2 * LANES] + acc[:, 2 * LANES :]


def gather_rows(indices, table_row, table_rows):
    high = lax.shift_right_arithmetic(indices, 7)
    low = jnp.bitwise_and(indices, LANES - 1)
    acc = [jnp.zeros(indices.shape, F32) for _ in range(2)]
    for a in range(table_rows):
        row = jnp.broadcast_to(table_row(a), indices.shape)
        picked = jnp.take_along_axis(row, low, axis=1, mode="promise_in_bounds")
        acc[a % 2] = jnp.where(high == a, picked, acc[a % 2])
    return acc[0] + acc[1]


def store_digits(idx, high_ref, low_ref):
    high_ref[...] = lax.shift_right_arithmetic(idx, 7).astype(F32)
    low_ref[...] = jnp.bitwise_and(idx, LANES - 1).astype(F32)


def floor_div(value, divisor):
    return jnp.floor((value + 0.5) * (1.0 / divisor))


def cell_digits(cells):
    cells = cells.astype(F32)
    plane = floor_div(cells, 252)
    spot = cells - 252.0 * plane
    slot = (
        spot
        + jnp.where(spot >= 64.0, 1.0, 0.0)
        + jnp.where(spot >= 126.0, 2.0, 0.0)
        + jnp.where(spot >= 188.0, 1.0, 0.0)
    )
    along_x = floor_div(plane, 12)
    rest = plane - 12.0 * along_x
    patch = floor_div(rest, 3)
    component = rest - 3.0 * patch
    half = jnp.where(slot >= 128.0, 1.0, 0.0)
    return patch, component, along_x, half, slot - 128.0 * half


def own_lanes():
    lane = lax.broadcasted_iota(jnp.int32, (1, LANES), 1)
    return lax.shift_right_logical(lane, 5)


def spread_lanes(row):
    return jnp.concatenate([row] * 4, axis=1)


CHUNK = 64
WIDE = 192
LOAD_ROWS = 34
SLAB_ROWS = 40
OWNER_ROWS = 14


def start_copies(pairs, sems):
    copies = [
        pltpu.make_async_copy(source, target, sems.at[n])
        for n, (source, target) in enumerate(pairs)
    ]
    for copy in copies:
        copy.start()
    return copies


def back_kernel(
    pair_hbm, dir_hbm, cells_hbm, prim_hbm, ids_hbm, basis_hbm, values_hbm, coeff_hbm,
    out_ref, idx_ref, cells_ref, small_ref, bxt_ref, bx_ref, bdt_ref, bd_ref, cst_ref,
    pair_ref, dir_ref, prim_ref, ids_ref, basis_ref, values_ref, coeff_ref,
    high_ref, low_ref, piece_ref, acc_ref, sems,
):
    pencil = lax.axis_index("pencil")
    patch = lax.div(pencil, 2)
    side = lax.rem(pencil, 2)
    copies = start_copies(
        [
            (pair_hbm, pair_ref),
            (dir_hbm, dir_ref),
            (cells_hbm, cells_ref),
            (prim_hbm, prim_ref),
            (ids_hbm, ids_ref),
            (basis_hbm.at[patch], basis_ref),
            (values_hbm, values_ref),
            (coeff_hbm, coeff_ref),
        ],
        sems,
    )
    half = dir_ref.shape[0]
    for ref in (bx_ref, bxt_ref, bd_ref, bdt_ref):
        ref[...] = jnp.zeros(ref.shape, BF16)
    copies[0].wait()
    copies[1].wait()
    for k in range(half):
        both = pair_ref[:, k * LANES : (k + 1) * LANES]
        idx_ref[k : k + 1, :] = both[0:1]
        idx_ref[half + k : half + k + 1, :] = both[1:2]
    store_digits(idx_ref[...], high_ref, low_ref)
    for n, piece in enumerate(split_channels(dir_ref[...], 2)):
        piece_ref[n, :half, :] = piece
        piece_ref[n, half:, :] = -piece
    acc_ref[...] = scatter_large(
        WIDE,
        high_ref,
        low_ref,
        lambda n, t, r: piece_ref[n, pl.ds(t * CHUNK + r, 1), :],
        2 * half,
        CHUNK,
    )
    out_ref[...] = acc_ref[: 2 * half, :]
    for copy in copies[2:]:
        copy.wait()
    small_ref[...] = jnp.zeros(small_ref.shape, F32)
    small_ref[0:1, :] = spread_lanes(prim_ref[...].astype(F32))
    small_ref[1:2, :] = spread_lanes(ids_ref[...].astype(F32))
    along_x, along_y, along_z = basis_ref[0], basis_ref[1], basis_ref[2]
    first = lax.broadcasted_iota(jnp.int32, (64, 64), 0)
    second = lax.broadcasted_iota(jnp.int32, (64, 64), 1)
    identity = jnp.where(first == second, 1.0, 0.0)
    half_x = jnp.where(side == 1, along_x[:, 32:64], along_x[:, 0:32])
    flipped = full_dot(identity, along_x, ((1,), (1,)))
    half_flipped = jnp.where(side == 1, flipped[32:64], flipped[0:32])
    flipped_y = full_dot(identity, along_y, ((1,), (1,)))
    flipped_z = full_dot(identity, along_z, ((1,), (1,)))
    store_left(bx_ref, 128, [(0, 0, along_x), (64, 64, half_x)])
    store_left(bxt_ref, 128, [(0, 0, flipped), (64, 64, half_flipped)])
    store_left(bd_ref, 256, diagonal(along_z, along_y))
    store_left(bdt_ref, 256, diagonal(flipped_z, flipped_y))

    def spread(column):
        return jnp.broadcast_to(column, (64, LANES))

    cst_ref[0] = spread(column_of(along_y[0:1]))
    cst_ref[1] = spread(column_of(along_y[63:64]))
    cst_ref[2] = spread(column_of(along_z[0:1]))
    cst_ref[3] = spread(column_of(along_z[63:64]))
    lane = lax.broadcasted_iota(jnp.int32, (1, LANES), 1)

    def weight(dim):
        own = jnp.where(
            side == 1, coeff_ref[2, pl.ds(patch, 1), :], coeff_ref[0, pl.ds(patch, 1), :]
        )
        shared = coeff_ref[1, pl.ds(patch, 1), :]
        own, shared = (
            jnp.broadcast_to(value[:, dim : dim + 1], (1, LANES)) for value in (own, shared)
        )
        return jnp.where(lane < 64, own, jnp.where(lane < 96, shared, 0.0))

    x_values, y_values, z_values = (values_ref[dim, pl.ds(patch, 1), :] for dim in range(3))
    half_values = jnp.where(side == 1, x_values[:, 32:64], x_values[:, 0:32])
    lane_values = jnp.concatenate([x_values, half_values, half_values], axis=1)
    x_term = jnp.where(lane >= 96, 1.0, weight(0) * lane_values)
    y_term = weight(1) * spread(column_of(y_values))
    cst_ref[4] = x_term + y_term
    cst_ref[5] = weight(2) * spread(column_of(z_values))


def load_kernel(
    arr_ref, pos_ref, small_ref, out_ref, slots_ref, high_ref, low_ref, piece_ref, acc_ref
):
    patch, component, along_x, half, lane = cell_digits(pos_ref[...])
    row = patch * 48.0 + half * 24.0 + component * 8.0 + along_x
    high_ref[...] = row
    low_ref[...] = lane
    slots_ref[...] = (row * 128.0 + lane).astype(jnp.int32)
    rows = pos_ref.shape[0]
    for n, piece in enumerate(split_channels(arr_ref[...], 2)):
        piece_ref[n] = piece
    acc_ref[...] = scatter_large(
        acc_ref.shape[0],
        high_ref,
        low_ref,
        lambda n, t, r: piece_ref[n, pl.ds(t * CHUNK + r, 1), :],
        rows,
        CHUNK,
    )
    pencil = lax.axis_index("pencil")
    mine = own_lanes() == lax.rem(pencil, 4)
    primal = jnp.broadcast_to(small_ref[0:1, :], (8, LANES)).astype(jnp.int32)
    cells = gather_rows(primal, lambda a: pos_ref[a : a + 1, :].astype(F32), rows)
    patch, component, along_x, half, lane = cell_digits(cells[0:1])
    place = half * 128.0 + along_x + (8 * pencil).astype(F32)
    code = place * 128.0 + lane
    ids = jnp.where(mine, small_ref[1:2, :], 0.0)
    for dest in range(out_ref.shape[0] // LOAD_ROWS):
        base = LOAD_ROWS * dest
        own = 2 * (dest % 2)
        for side in range(2):
            start = (dest // 2) * 48 + side * 24
            for n, c in enumerate((own, 1)):
                out_ref[base + side * 16 + 8 * n : base + side * 16 + 8 * n + 8, :] = acc_ref[
                    start + 8 * c : start + 8 * c + 8, :
                ]
        here = jnp.where(
            component == float(own), code, jnp.where(component == 1.0, code + 8192.0, -1.0)
        )
        here = jnp.where(patch == float(dest // 2), here, -1.0)
        out_ref[base + 32 : base + 33, :] = jnp.where(mine, here, 0.0)
        out_ref[base + 33 : base + 34, :] = ids


def full_dot(left, right, contract):
    return lax.dot_general(
        left, right, ((contract[0], contract[1]), ((), ())), precision=HIGHEST,
        preferred_element_type=F32,
    )


def split_pair(value):
    high = value.astype(BF16)
    return high, (value - high.astype(F32)).astype(BF16)


def store_left(ref, width, blocks):
    for row, lane, block in blocks:
        high, low = split_pair(block)
        for n, piece in enumerate((high, high, low)):
            start = n * width + lane
            ref[row : row + block.shape[0], start : start + block.shape[1]] = piece


def diagonal(outer, inner):
    return [(64 * n, 64 * n, block) for n, block in enumerate((outer, inner, inner, outer))]


def split_dot(left_ref, right, contract_right):
    high, low = split_pair(right)
    return lax.dot_general(
        left_ref[...],
        jnp.concatenate([high, low, high], axis=contract_right),
        (((1,), (contract_right,)), ((), ())),
        preferred_element_type=F32,
    )


def column_of(row):
    count = row.shape[1]
    first = lax.broadcasted_iota(jnp.int32, (count, count), 0)
    second = lax.broadcasted_iota(jnp.int32, (count, count), 1)
    spread = jnp.broadcast_to(row, (count, count))
    return jnp.sum(jnp.where(first == second, spread, 0.0), axis=1, keepdims=True)


def solve_kernel(
    recv_ref, bxt_ref, bx_ref, bdt_ref, bd_ref, cst_ref, out_ref, fwd_ref, d0_ref, d1_ref,
    slab_ref, high_ref, low_ref, piece_ref,
):
    sources = recv_ref.shape[0] // LOAD_ROWS
    load = jnp.concatenate(
        [
            jnp.concatenate(
                [
                    recv_ref[LOAD_ROWS * src + start : LOAD_ROWS * src + start + 8, :]
                    for start in (8 * n, 16 + 8 * n)
                ],
                axis=1,
            )
            for n in range(2)
            for src in range(sources)
        ],
        axis=0,
    )
    fwd_ref[...] = split_dot(bdt_ref, split_dot(bxt_ref, load, 0), 1)

    def step(j, carry):
        top, bottom = carry

        def row(index):
            return jnp.broadcast_to(cst_ref[index, pl.ds(j, 1), :], (64, LANES))

        first = jnp.broadcast_to(fwd_ref[pl.ds(64 + j, 1), :], (64, LANES))
        last = jnp.broadcast_to(fwd_ref[pl.ds(128 + j, 1), :], (64, LANES))
        y_first, y_last = row(0), row(1)
        spectral = (
            y_first * fwd_ref[0:64, :]
            + y_last * fwd_ref[192:256, :]
            + first * cst_ref[2]
            + last * cst_ref[3]
        )
        scaled = spectral / (row(4) + cst_ref[5])
        along_first = cst_ref[2] * scaled
        along_last = cst_ref[3] * scaled
        d0_ref[j] = jnp.sum(along_first.reshape(8, 8, LANES), axis=0)
        d1_ref[j] = jnp.sum(along_last.reshape(8, 8, LANES), axis=0)
        return top + y_first * scaled, bottom + y_last * scaled

    zero = jnp.zeros((64, LANES), F32)
    top, bottom = lax.fori_loop(0, 64, step, (zero, zero), unroll=4)
    edges = jnp.concatenate(
        [top, jnp.sum(d0_ref[...], axis=1), jnp.sum(d1_ref[...], axis=1), bottom], axis=0
    )
    slab_ref[...] = split_dot(bx_ref, split_dot(bd_ref, edges, 0), 1)

    def packed(row):
        halves = []
        for part in range(2):
            starts = [LOAD_ROWS * (4 * part + k) + row for k in range(4)]
            value = recv_ref[starts[0] : starts[0] + 1, :]
            for start in starts[1:]:
                value = value + recv_ref[start : start + 1, :]
            halves.append(value)
        return jnp.concatenate(halves + [jnp.full((6, LANES), -1.0, F32)], axis=0)

    codes = packed(32).astype(jnp.int32)
    ids = packed(33).astype(jnp.int32)
    primal = gather_rows(
        codes,
        lambda a: slab_ref[a % 128 : a % 128 + 1, (a // 128) * LANES : (a // 128 + 1) * LANES],
        256,
    )
    store_digits(ids, high_ref, low_ref)
    for n, piece in enumerate(split_channels(primal, 3)):
        piece_ref[n] = piece
    partial = scatter_small(16, high_ref, low_ref, piece_ref, 2)
    for dest in range(out_ref.shape[0] // SLAB_ROWS):
        base = SLAB_ROWS * dest
        for half in range(2):
            lanes = slice(half * LANES, (half + 1) * LANES)
            for n in range(2):
                start = base + 16 * half + 8 * n
                out_ref[start : start + 8, :] = slab_ref[
                    64 * n + 8 * dest : 64 * n + 8 * dest + 8, lanes
                ]
        out_ref[base + 32 : base + 40, :] = partial[0:8, :]


def pick_kernel(
    recv_ref, idx_ref, small_ref, inv_hbm, out_ref, table_ref, pick_ref, inv_ref, mid_ref,
    lift_ref, sem,
):
    copy = pltpu.make_async_copy(inv_hbm, inv_ref, sem)
    copy.start()
    sources = recv_ref.shape[0] // SLAB_ROWS

    def block_of(src, start):
        return recv_ref[SLAB_ROWS * src + start : SLAB_ROWS * src + start + 8, :]

    coarse = block_of(0, 32)
    for src in range(1, sources):
        coarse = coarse + block_of(src, 32)
    for p in range(sources // 2):
        for half in range(2):
            start = p * 48 + half * 24
            table_ref[start : start + 8, :] = block_of(2 * p, 16 * half)
            table_ref[start + 8 : start + 16, :] = block_of(2 * p, 16 * half + 8) + block_of(
                2 * p + 1, 16 * half + 8
            )
            table_ref[start + 16 : start + 24, :] = block_of(2 * p + 1, 16 * half)
    table_rows = table_ref.shape[0]

    def block(t, carry):
        for sub in range(4):
            start = pl.multiple_of(t * 32 + sub * 8, 8)
            pick_ref[pl.ds(start, 8), :] = gather_rows(
                idx_ref[pl.ds(start, 8), :], lambda a: table_ref[a : a + 1, :], table_rows
            )
        return carry

    lax.fori_loop(0, 4, block, 0)
    mid_ref[...] = coarse
    copy.wait()
    coarse_rows = [jnp.broadcast_to(mid_ref[q : q + 1, :], (LANES, LANES)) for q in range(8)]
    ones = jnp.ones((16, LANES), BF16)
    for part in range(8):
        rows = slice(part * LANES, (part + 1) * LANES)
        product = inv_ref[rows, 0:LANES] * coarse_rows[0]
        for q in range(1, 8):
            product = product + inv_ref[rows, q * LANES : (q + 1) * LANES] * coarse_rows[q]
        high, low = split_pair(product)
        lift_ref[part : part + 1, :] = (pair_dot(ones, high) + pair_dot(ones, low))[0:1]
    lift = lift_ref[...]
    mine = own_lanes() == lax.rem(lax.axis_index("group"), 4)
    extra = jnp.where(mine, small_ref[0:2, :], 0.0)
    for h in range(pick_ref.shape[0] // 4):
        start = OWNER_ROWS * h
        out_ref[start : start + 8, :] = lift
        out_ref[start + 8 : start + 12, :] = pick_ref[4 * h : 4 * h + 4, :]
        out_ref[start + 12 : start + 14, :] = extra


def image_kernel(
    own_ref, pair_ref, dir_hbm, res_hbm, scale_hbm, iterate_hbm,
    image_ref, sums_ref, dir_ref, res_ref, scale_ref, iterate_ref,
    lift_ref, high_ref, low_ref, piece_ref, corr_ref, table_ref, sems,
):
    copies = start_copies(
        [
            (dir_hbm, dir_ref),
            (res_hbm, res_ref),
            (scale_hbm, scale_ref),
            (iterate_hbm, iterate_ref),
        ],
        sems,
    )
    groups = own_ref.shape[0] // OWNER_ROWS
    total = own_ref[0:8, :]
    for h in range(1, groups):
        total = total + own_ref[OWNER_ROWS * h : OWNER_ROWS * h + 8, :]
    lift_ref[...] = total

    def packed(row):
        rows = []
        for q in range(8):
            start = OWNER_ROWS * 4 * q + row
            value = own_ref[start : start + 1, :]
            for k in range(1, 4):
                start = OWNER_ROWS * (4 * q + k) + row
                value = value + own_ref[start : start + 1, :]
            rows.append(value)
        return jnp.concatenate(rows, axis=0).astype(jnp.int32)

    local = packed(12) - 512 * lax.axis_index("group")
    ids = packed(13)
    sender = 4 * lax.broadcasted_iota(jnp.int32, (8, LANES), 0) + jnp.broadcast_to(
        own_lanes(), (8, LANES)
    )
    valid = jnp.logical_and(local >= 0, local < 512)
    store_digits(jnp.where(valid, sender * 512 + local, -1), high_ref, low_ref)

    lifted = gather_rows(ids, lambda a: lift_ref[a : a + 1, :], 8)
    for n, piece in enumerate(split_channels(lifted, 3)):
        piece_ref[n] = piece
    corr_ref[...] = scatter_small(4 * groups, high_ref, low_ref, piece_ref, 8)
    for h in range(groups):
        start = OWNER_ROWS * h + 8
        table_ref[4 * h : 4 * h + 4, :] = (
            own_ref[start : start + 4, :] + corr_ref[4 * h : 4 * h + 4, :]
        )
    for copy in copies:
        copy.wait()

    half = dir_ref.shape[0]
    table_rows = 4 * groups

    def block(t, sums):
        sums = list(sums)
        for sub in range(2):
            start = pl.multiple_of(t * 16 + sub * 8, 8)
            plus, minus = (
                gather_rows(
                    pair_ref[pl.ds(base + start, 8), :],
                    lambda a: table_ref[a : a + 1, :],
                    table_rows,
                )
                for base in (0, half)
            )
            image = plus - minus
            image_ref[pl.ds(start, 8), :] = image
            res = res_ref[pl.ds(start, 8), :]
            scaled = scale_ref[pl.ds(start, 8), :]
            scaled_res = res * scaled
            sums[0] = sums[0] + scaled_res * res
            sums[1] = sums[1] + dir_ref[pl.ds(start, 8), :] * image
            sums[2] = sums[2] + scaled_res * image
            sums[3] = sums[3] + (scaled * image) * image
        return tuple(sums)

    zero = jnp.zeros((8, LANES), F32)
    sums = lax.fori_loop(0, half // 16, block, (zero, zero, zero, zero))
    lane = lax.broadcasted_iota(jnp.int32, (8, LANES), 1)
    packed_sums = jnp.zeros((8, LANES), F32)
    for n, part in enumerate(sums):
        value = jnp.sum(jnp.sum(part, axis=0, keepdims=True), axis=1, keepdims=True)
        packed_sums = jnp.where(lane == n, jnp.broadcast_to(value, (8, LANES)), packed_sums)
    for t in range(sums_ref.shape[0] // 8):
        sums_ref[8 * t : 8 * t + 8, :] = packed_sums


def update_kernel(
    sums_ref, dir_ref, res_ref, scale_ref, iterate_ref, image_ref, it_out, res_out, dir_out
):
    totals = jnp.sum(sums_ref[...], axis=0, keepdims=True)
    lane = lax.broadcasted_iota(jnp.int32, (1, LANES), 1)

    def pick(n):
        return jnp.sum(jnp.where(lane == n, totals, 0.0), axis=1, keepdims=True)

    old, curvature, cross, square = pick(0), pick(1), pick(2), pick(3)
    alpha = old / curvature
    new = old - 2.0 * alpha * cross + (alpha * alpha) * square
    beta = new / old
    direction = dir_ref[...]
    res_next = res_ref[...] - alpha * image_ref[...]
    it_out[...] = iterate_ref[...] + alpha * direction
    res_out[...] = res_next
    dir_out[...] = scale_ref[...] * res_next + beta * direction


def exchange(array, axis):
    return lax.all_to_all(array, axis, split_axis=0, concat_axis=0, tiled=True)


def f32(*shape):
    return jax.ShapeDtypeStruct(shape, F32)


def i32(*shape):
    return jax.ShapeDtypeStruct(shape, jnp.int32)


def body(
    mult_iterate,
    residual,
    direction,
    mult_scale,
    eigen_basis,
    eigen_values,
    elastic_coef,
    coarse_inverse,
    send_pos,
    pair_slots,
    prim_rows,
    coarse_idx,
):
    groups = lax.axis_size("group")
    pencils = lax.axis_size("pencil")
    iterate_now = mult_iterate.reshape(64, LANES)
    resid_now = residual.reshape(64, LANES)
    search_dir = direction.reshape(64, LANES)
    scale_now = mult_scale.reshape(64, LANES)
    cells = send_pos.reshape(128, LANES)
    pairs = pair_slots.reshape(2, 8192)
    primal = prim_rows.reshape(1, 32)
    coarse_ids = coarse_idx.reshape(1, 32)

    def resident(array):
        return pltpu.with_memory_space_constraint(array, pltpu.HBM)

    digits = [pltpu.VMEM((128, LANES), F32), pltpu.VMEM((128, LANES), F32)]
    pieces = pltpu.VMEM((2, 128, LANES), F32)
    small = [
        pltpu.VMEM((8, LANES), F32),
        pltpu.VMEM((8, LANES), F32),
        pltpu.VMEM((3, 8, LANES), F32),
    ]
    sources = (
        pairs,
        search_dir,
        cells,
        primal,
        coarse_ids,
        eigen_basis,
        eigen_values.transpose(1, 0, 2),
        elastic_coef.transpose(1, 0, 2),
    )
    back, pair_rows, cells, primals, *constants = call(
        back_kernel,
        (
            f32(128, LANES),
            i32(128, LANES),
            i32(128, LANES),
            f32(8, LANES),
            jax.ShapeDtypeStruct((128, 384), BF16),
            jax.ShapeDtypeStruct((128, 384), BF16),
            jax.ShapeDtypeStruct((256, 768), BF16),
            jax.ShapeDtypeStruct((256, 768), BF16),
            f32(6, 64, LANES),
        ),
        [HBM] * len(sources),
        "back",
        [
            pltpu.VMEM((2, 8192), jnp.int32),
            pltpu.VMEM((64, LANES), F32),
            pltpu.VMEM((1, 32), jnp.int32),
            pltpu.VMEM((1, 32), jnp.int32),
            pltpu.VMEM((3, 64, 64), F32),
            pltpu.VMEM((3, 4, 64), F32),
            pltpu.VMEM((3, 4, 3), F32),
        ]
        + digits
        + [pieces, pltpu.VMEM((WIDE, LANES), F32), pltpu.SemaphoreType.DMA((len(sources),))],
    )(*(resident(source) for source in sources))
    arrived = exchange(back.reshape(groups, 4, LANES), "group").reshape(128, LANES)

    loads, slots = call(
        load_kernel,
        (f32(pencils * LOAD_ROWS, LANES), i32(128, LANES)),
        [VMEM] * 3,
        "load",
        digits + [pieces, pltpu.VMEM((192, LANES), F32)],
    )(arrived, cells, primals)
    columns = exchange(loads.reshape(pencils, 1, LOAD_ROWS * LANES), "pencil")

    partial = call(
        solve_kernel,
        f32(pencils * SLAB_ROWS, LANES),
        [VMEM] * 6,
        "solve",
        [
            pltpu.VMEM((256, LANES), F32),
            pltpu.VMEM((64, 8, LANES), F32),
            pltpu.VMEM((64, 8, LANES), F32),
            pltpu.VMEM((128, 256), F32),
        ]
        + small,
    )(columns.reshape(pencils * LOAD_ROWS, LANES), *constants)
    slabs = exchange(partial.reshape(pencils, 1, SLAB_ROWS * LANES), "pencil")

    picked = call(
        pick_kernel,
        f32(groups * OWNER_ROWS, LANES),
        [VMEM, VMEM, VMEM, HBM],
        "pick",
        [
            pltpu.VMEM((192, LANES), F32),
            pltpu.VMEM((128, LANES), F32),
            pltpu.VMEM((1024, 1024), F32),
            pltpu.VMEM((8, LANES), F32),
            pltpu.VMEM((8, LANES), F32),
            pltpu.SemaphoreType.DMA,
        ],
    )(slabs.reshape(pencils * SLAB_ROWS, LANES), slots, primals, resident(coarse_inverse))
    owner = exchange(picked.reshape(groups, 1, OWNER_ROWS * LANES), "group")

    shape = f32(64, LANES)
    image, sums, *vectors = call(
        image_kernel,
        (shape, f32(groups * pencils, LANES), shape, shape, shape, shape),
        [VMEM, VMEM] + [HBM] * 4,
        "image",
        [pltpu.VMEM((8, LANES), F32)]
        + small
        + [
            pltpu.VMEM((128, LANES), F32),
            pltpu.VMEM((128, LANES), F32),
            pltpu.SemaphoreType.DMA((4,)),
        ],
    )(
        owner.reshape(groups * OWNER_ROWS, LANES),
        pair_rows,
        *(resident(array) for array in (search_dir, resid_now, scale_now, iterate_now)),
    )
    totals = exchange(sums, ("group", "pencil"))

    outs = call(update_kernel, (shape, shape, shape), [VMEM] * 6, "update")(
        totals, *vectors, image
    )
    return tuple(out.reshape(1, 1, -1) for out in outs)


def solution(mesh):
    in_specs = (
        P("group", "pencil", None),
        P("group", "pencil", None),
        P("group", "pencil", None),
        P("group", "pencil", None),
        P("group", None, None, None),
        P("group", None, None),
        P("group", None, None),
        P(),
        P("group", "pencil", None),
        P("group", "pencil", None, None),
        P("group", "pencil", None),
        P("group", "pencil", None),
    )
    out_specs = (P("group", "pencil", None), P("group", "pencil", None), P("group", "pencil", None))
    return jax.shard_map(body, mesh=mesh, in_specs=in_specs, out_specs=out_specs, check_vma=False)
```

```python
import jax
import jax.numpy as jnp
from jax import lax
from jax.experimental import pallas as pl
from jax.experimental.pallas import tpu as pltpu
from jax.sharding import PartitionSpec as P

LANES = 128
BF16 = jnp.bfloat16
F32 = jnp.float32
HIGHEST = lax.Precision.HIGHEST
VMEM = pl.BlockSpec(memory_space=pltpu.VMEM)


HBM = pl.BlockSpec(memory_space=pltpu.HBM)


def call(kernel, out_shape, in_specs, name, scratch=(), flops=4_000_000):
    single = not isinstance(out_shape, (tuple, list))
    return pl.pallas_call(
        kernel,
        out_shape=out_shape,
        in_specs=in_specs,
        out_specs=VMEM if single else [VMEM] * len(out_shape),
        scratch_shapes=list(scratch),
        name=name,
        compiler_params=pltpu.CompilerParams(vmem_limit_bytes=16 << 20),
        cost_estimate=pl.CostEstimate(flops=flops, bytes_accessed=1 << 18, transcendentals=0),
    )


def split_channels(value, count):
    pieces = []
    for _ in range(count):
        piece = value.astype(BF16).astype(F32)
        pieces.append(piece)
        value = value - piece
    return pieces


def one_hot_parts(rows, high_row, low_row, piece_rows, chunk, channels):
    row_ids = lax.broadcasted_iota(jnp.int32, (rows, LANES), 0).astype(F32).astype(BF16)
    lane_ids = lax.broadcasted_iota(jnp.int32, (LANES, LANES), 0).astype(F32).astype(BF16)
    left, right = [], []
    for r in range(chunk):
        high = jnp.broadcast_to(high_row(r), (rows, LANES)).astype(BF16)
        low = jnp.broadcast_to(low_row(r), (LANES, LANES)).astype(BF16)
        left.append(jnp.where(row_ids == high, BF16(1), BF16(0)))
        match = lane_ids == low
        pieces = [
            jnp.where(
                match, jnp.broadcast_to(piece_rows(n, r), (LANES, LANES)).astype(BF16), BF16(0)
            )
            for n in range(channels)
        ]
        right.append(jnp.concatenate(pieces, axis=0))
    return jnp.concatenate(left, axis=1), jnp.concatenate(right, axis=1)


def pair_dot(left, right):
    return lax.dot_general(left, right, (((1,), (1,)), ((), ())), preferred_element_type=F32)


def scatter_large(rows, high_ref, low_ref, piece_row, total, chunk):
    def step(index, acc):
        left, right = one_hot_parts(
            rows,
            lambda r: high_ref[pl.ds(index * chunk + r, 1), :],
            lambda r: low_ref[pl.ds(index * chunk + r, 1), :],
            lambda n, r: piece_row(n, index, r),
            chunk,
            2,
        )
        return acc + pair_dot(right, left)

    acc = lax.fori_loop(0, total // chunk, step, jnp.zeros((2 * LANES, rows), F32))
    return (acc[:LANES] + acc[LANES:]).T


def scatter_small(rows, high_ref, low_ref, piece_ref, count):
    left, right = one_hot_parts(
        rows,
        lambda r: high_ref[r : r + 1, :],
        lambda r: low_ref[r : r + 1, :],
        lambda n, r: piece_ref[n, r : r + 1, :],
        count,
        3,
    )
    acc = pair_dot(left, right)
    return acc[:, :LANES] + acc[:, LANES : 2 * LANES] + acc[:, 2 * LANES :]


def gather_rows(indices, table_row, table_rows):
    high = lax.shift_right_arithmetic(indices, 7)
    low = jnp.bitwise_and(indices, LANES - 1)
    acc = [jnp.zeros(indices.shape, F32) for _ in range(2)]
    for a in range(table_rows):
        row = jnp.broadcast_to(table_row(a), indices.shape)
        picked = jnp.take_along_axis(row, low, axis=1, mode="promise_in_bounds")
        acc[a % 2] = jnp.where(high == a, picked, acc[a % 2])
    return acc[0] + acc[1]


def gather_mixed(idx_ref, table_ref, out_ref, flip_ref, high_ref, low_ref, permuted, matched):
    table_rows = table_ref.shape[0]
    flipped = table_ref[...].T
    flip_ref[...] = jnp.concatenate(split_pair(flipped), axis=1)
    store_digits(idx_ref[...], high_ref, low_ref)
    row_ids = lax.broadcasted_iota(jnp.int32, (table_rows, LANES), 0).astype(F32).astype(BF16)
    lane_ids = lax.broadcasted_iota(jnp.int32, (LANES, LANES), 0).astype(F32)
    step = permuted * 8 + matched

    def block(t, carry):
        base = t * step
        second = base + permuted * 8
        select = []
        for r in range(matched):
            high = jnp.broadcast_to(high_ref[pl.ds(second + r, 1), :], (table_rows, LANES))
            select.append(jnp.where(row_ids == high.astype(BF16), BF16(1), BF16(0)))
        select = jnp.concatenate(select, axis=1)
        for sub in range(permuted):
            start = pl.multiple_of(base + 8 * sub, 8)
            out_ref[pl.ds(start, 8), :] = gather_rows(
                idx_ref[pl.ds(start, 8), :], lambda a: table_ref[a : a + 1, :], table_rows
            )
        rows = lax.dot_general(
            flip_ref[...],
            jnp.concatenate([select, select], axis=0),
            (((1,), (0,)), ((), ())),
            preferred_element_type=F32,
        )
        picked = []
        for r in range(matched):
            low = jnp.broadcast_to(low_ref[pl.ds(second + r, 1), :], (LANES, LANES))
            own = jnp.where(lane_ids == low, rows[:, r * LANES : (r + 1) * LANES], 0.0)
            picked.append(jnp.sum(own, axis=0, keepdims=True))
        out_ref[pl.ds(pl.multiple_of(second, 8), matched), :] = jnp.concatenate(picked, axis=0)
        return carry

    lax.fori_loop(0, idx_ref.shape[0] // step, block, 0)


def store_digits(idx, high_ref, low_ref):
    high_ref[...] = lax.shift_right_arithmetic(idx, 7).astype(F32)
    low_ref[...] = jnp.bitwise_and(idx, LANES - 1).astype(F32)


def floor_div(value, divisor):
    return jnp.floor((value + 0.5) * (1.0 / divisor))


def cell_digits(cells):
    cells = cells.astype(F32)
    plane = floor_div(cells, 252)
    spot = cells - 252.0 * plane
    slot = (
        spot
        + jnp.where(spot >= 64.0, 1.0, 0.0)
        + jnp.where(spot >= 126.0, 2.0, 0.0)
        + jnp.where(spot >= 188.0, 1.0, 0.0)
    )
    along_x = floor_div(plane, 12)
    rest = plane - 12.0 * along_x
    patch = floor_div(rest, 3)
    component = rest - 3.0 * patch
    half = jnp.where(slot >= 128.0, 1.0, 0.0)
    return patch, component, along_x, half, slot - 128.0 * half


def own_lanes():
    lane = lax.broadcasted_iota(jnp.int32, (1, LANES), 1)
    return lax.shift_right_logical(lane, 5)


def spread_lanes(row):
    return jnp.concatenate([row] * 4, axis=1)


CHUNK = 64
WIDE = 192
LOAD_ROWS = 34
SLAB_ROWS = 40
OWNER_ROWS = 14


def start_copies(pairs, sems):
    copies = [
        pltpu.make_async_copy(source, target, sems.at[n])
        for n, (source, target) in enumerate(pairs)
    ]
    for copy in copies:
        copy.start()
    return copies


def back_kernel(
    pair_hbm, dir_hbm, cells_hbm, prim_hbm, ids_hbm, basis_hbm, values_hbm, coeff_hbm,
    out_ref, idx_ref, cells_ref, small_ref, basis_ref, values_ref, coeff_ref,
    pair_ref, dir_ref, prim_ref, ids_ref,
    high_ref, low_ref, piece_ref, acc_ref, sems,
):
    patch = lax.div(lax.axis_index("pencil"), 2)
    copies = start_copies(
        [
            (pair_hbm, pair_ref),
            (dir_hbm, dir_ref),
            (cells_hbm, cells_ref),
            (prim_hbm, prim_ref),
            (ids_hbm, ids_ref),
            (basis_hbm.at[patch], basis_ref),
            (values_hbm, values_ref),
            (coeff_hbm, coeff_ref),
        ],
        sems,
    )
    half = dir_ref.shape[0]
    copies[0].wait()
    copies[1].wait()
    for k in range(half):
        both = pair_ref[:, k * LANES : (k + 1) * LANES]
        idx_ref[k : k + 1, :] = both[0:1]
        idx_ref[half + k : half + k + 1, :] = both[1:2]
    store_digits(idx_ref[...], high_ref, low_ref)
    for n, piece in enumerate(split_channels(dir_ref[...], 2)):
        piece_ref[n, :half, :] = piece
        piece_ref[n, half:, :] = -piece
    acc_ref[...] = scatter_large(
        WIDE,
        high_ref,
        low_ref,
        lambda n, t, r: piece_ref[n, pl.ds(t * CHUNK + r, 1), :],
        2 * half,
        CHUNK,
    )
    out_ref[...] = acc_ref[: 2 * half, :]
    for copy in copies[2:]:
        copy.wait()
    small_ref[...] = jnp.zeros(small_ref.shape, F32)
    small_ref[0:1, :] = spread_lanes(prim_ref[...].astype(F32))
    small_ref[1:2, :] = spread_lanes(ids_ref[...].astype(F32))


def load_kernel(
    arr_ref, pos_ref, small_ref, out_ref, slots_ref, high_ref, low_ref, piece_ref, acc_ref
):
    patch, component, along_x, half, lane = cell_digits(pos_ref[...])
    row = patch * 48.0 + half * 24.0 + component * 8.0 + along_x
    high_ref[...] = row
    low_ref[...] = lane
    slots_ref[...] = (row * 128.0 + lane).astype(jnp.int32)
    rows = pos_ref.shape[0]
    for n, piece in enumerate(split_channels(arr_ref[...], 2)):
        piece_ref[n] = piece
    acc_ref[...] = scatter_large(
        acc_ref.shape[0],
        high_ref,
        low_ref,
        lambda n, t, r: piece_ref[n, pl.ds(t * CHUNK + r, 1), :],
        rows,
        CHUNK,
    )
    pencil = lax.axis_index("pencil")
    mine = own_lanes() == lax.rem(pencil, 4)
    primal = jnp.broadcast_to(small_ref[0:1, :], (8, LANES)).astype(jnp.int32)
    cells = gather_rows(primal, lambda a: pos_ref[a : a + 1, :].astype(F32), rows)
    patch, component, along_x, half, lane = cell_digits(cells[0:1])
    place = half * 128.0 + along_x + (8 * pencil).astype(F32)
    code = place * 128.0 + lane
    ids = jnp.where(mine, small_ref[1:2, :], 0.0)
    for dest in range(out_ref.shape[0] // LOAD_ROWS):
        base = LOAD_ROWS * dest
        own = 2 * (dest % 2)
        for side in range(2):
            start = (dest // 2) * 48 + side * 24
            for n, c in enumerate((own, 1)):
                out_ref[base + side * 16 + 8 * n : base + side * 16 + 8 * n + 8, :] = acc_ref[
                    start + 8 * c : start + 8 * c + 8, :
                ]
        here = jnp.where(
            component == float(own), code, jnp.where(component == 1.0, code + 8192.0, -1.0)
        )
        here = jnp.where(patch == float(dest // 2), here, -1.0)
        out_ref[base + 32 : base + 33, :] = jnp.where(mine, here, 0.0)
        out_ref[base + 33 : base + 34, :] = ids


def full_dot(left, right, contract):
    return lax.dot_general(
        left, right, ((contract[0], contract[1]), ((), ())), precision=HIGHEST,
        preferred_element_type=F32,
    )


def split_pair(value):
    high = value.astype(BF16)
    return high, (value - high.astype(F32)).astype(BF16)


def store_left(ref, width, blocks):
    for row, lane, block in blocks:
        high, low = split_pair(block)
        for n, piece in enumerate((high, high, low)):
            start = n * width + lane
            ref[row : row + block.shape[0], start : start + block.shape[1]] = piece


def diagonal(outer, inner):
    return [(64 * n, 64 * n, block) for n, block in enumerate((outer, inner, inner, outer))]


def split_dot(left_ref, right, contract_right):
    high, low = split_pair(right)
    return lax.dot_general(
        left_ref[...],
        jnp.concatenate([high, low, high], axis=contract_right),
        (((1,), (contract_right,)), ((), ())),
        preferred_element_type=F32,
    )


def column_of(row):
    count = row.shape[1]
    first = lax.broadcasted_iota(jnp.int32, (count, count), 0)
    second = lax.broadcasted_iota(jnp.int32, (count, count), 1)
    spread = jnp.broadcast_to(row, (count, count))
    return jnp.sum(jnp.where(first == second, spread, 0.0), axis=1, keepdims=True)


def solve_kernel(
    recv_ref, basis_ref, values_ref, coeff_ref, out_ref, bxt_ref, bx_ref, bdt_ref, bd_ref, cst_ref,
    fwd_ref, d0_ref, d1_ref, slab_ref, high_ref, low_ref, piece_ref,
):
    pencil = lax.axis_index("pencil")
    patch = lax.div(pencil, 2)
    side = lax.rem(pencil, 2)
    for ref in (bx_ref, bxt_ref, bd_ref, bdt_ref):
        ref[...] = jnp.zeros(ref.shape, BF16)
    along_x, along_y, along_z = basis_ref[0], basis_ref[1], basis_ref[2]
    first = lax.broadcasted_iota(jnp.int32, (64, 64), 0)
    second = lax.broadcasted_iota(jnp.int32, (64, 64), 1)
    identity = jnp.where(first == second, 1.0, 0.0)
    half_x = jnp.where(side == 1, along_x[:, 32:64], along_x[:, 0:32])
    flipped = full_dot(identity, along_x, ((1,), (1,)))
    half_flipped = jnp.where(side == 1, flipped[32:64], flipped[0:32])
    flipped_y = full_dot(identity, along_y, ((1,), (1,)))
    flipped_z = full_dot(identity, along_z, ((1,), (1,)))
    store_left(bx_ref, 128, [(0, 0, along_x), (64, 64, half_x)])
    store_left(bxt_ref, 128, [(0, 0, flipped), (64, 64, half_flipped)])
    store_left(bd_ref, 256, diagonal(along_z, along_y))
    store_left(bdt_ref, 256, diagonal(flipped_z, flipped_y))

    def spread(column):
        return jnp.broadcast_to(column, (64, LANES))

    cst_ref[0] = spread(column_of(along_y[0:1]))
    cst_ref[1] = spread(column_of(along_y[63:64]))
    cst_ref[2] = spread(column_of(along_z[0:1]))
    cst_ref[3] = spread(column_of(along_z[63:64]))
    lane = lax.broadcasted_iota(jnp.int32, (1, LANES), 1)

    def weight(dim):
        own = jnp.where(
            side == 1, coeff_ref[2, pl.ds(patch, 1), :], coeff_ref[0, pl.ds(patch, 1), :]
        )
        shared = coeff_ref[1, pl.ds(patch, 1), :]
        own, shared = (
            jnp.broadcast_to(value[:, dim : dim + 1], (1, LANES)) for value in (own, shared)
        )
        return jnp.where(lane < 64, own, jnp.where(lane < 96, shared, 0.0))

    x_values, y_values, z_values = (values_ref[dim, pl.ds(patch, 1), :] for dim in range(3))
    half_values = jnp.where(side == 1, x_values[:, 32:64], x_values[:, 0:32])
    lane_values = jnp.concatenate([x_values, half_values, half_values], axis=1)
    x_term = jnp.where(lane >= 96, 1.0, weight(0) * lane_values)
    y_term = weight(1) * spread(column_of(y_values))
    cst_ref[4] = x_term + y_term
    cst_ref[5] = weight(2) * spread(column_of(z_values))

    sources = recv_ref.shape[0] // LOAD_ROWS
    load = jnp.concatenate(
        [
            jnp.concatenate(
                [
                    recv_ref[LOAD_ROWS * src + start : LOAD_ROWS * src + start + 8, :]
                    for start in (8 * n, 16 + 8 * n)
                ],
                axis=1,
            )
            for n in range(2)
            for src in range(sources)
        ],
        axis=0,
    )
    fwd_ref[...] = split_dot(bdt_ref, split_dot(bxt_ref, load, 0), 1)

    def step(j, carry):
        top, bottom = carry

        def row(index):
            return jnp.broadcast_to(cst_ref[index, pl.ds(j, 1), :], (64, LANES))

        first = jnp.broadcast_to(fwd_ref[pl.ds(64 + j, 1), :], (64, LANES))
        last = jnp.broadcast_to(fwd_ref[pl.ds(128 + j, 1), :], (64, LANES))
        y_first, y_last = row(0), row(1)
        spectral = (
            y_first * fwd_ref[0:64, :]
            + y_last * fwd_ref[192:256, :]
            + first * cst_ref[2]
            + last * cst_ref[3]
        )
        scaled = spectral / (row(4) + cst_ref[5])
        along_first = cst_ref[2] * scaled
        along_last = cst_ref[3] * scaled
        d0_ref[j] = jnp.sum(along_first.reshape(8, 8, LANES), axis=0)
        d1_ref[j] = jnp.sum(along_last.reshape(8, 8, LANES), axis=0)
        return top + y_first * scaled, bottom + y_last * scaled

    zero = jnp.zeros((64, LANES), F32)
    top, bottom = lax.fori_loop(0, 64, step, (zero, zero), unroll=4)
    edges = jnp.concatenate(
        [top, jnp.sum(d0_ref[...], axis=1), jnp.sum(d1_ref[...], axis=1), bottom], axis=0
    )
    slab_ref[...] = split_dot(bx_ref, split_dot(bd_ref, edges, 0), 1)

    def packed(row):
        halves = []
        for part in range(2):
            starts = [LOAD_ROWS * (4 * part + k) + row for k in range(4)]
            value = recv_ref[starts[0] : starts[0] + 1, :]
            for start in starts[1:]:
                value = value + recv_ref[start : start + 1, :]
            halves.append(value)
        return jnp.concatenate(halves + [jnp.full((6, LANES), -1.0, F32)], axis=0)

    codes = packed(32).astype(jnp.int32)
    ids = packed(33).astype(jnp.int32)
    primal = gather_rows(
        codes,
        lambda a: slab_ref[a % 128 : a % 128 + 1, (a // 128) * LANES : (a // 128 + 1) * LANES],
        256,
    )
    store_digits(ids, high_ref, low_ref)
    for n, piece in enumerate(split_channels(primal, 3)):
        piece_ref[n] = piece
    partial = scatter_small(16, high_ref, low_ref, piece_ref, 2)
    for dest in range(out_ref.shape[0] // SLAB_ROWS):
        base = SLAB_ROWS * dest
        for half in range(2):
            lanes = slice(half * LANES, (half + 1) * LANES)
            for n in range(2):
                start = base + 16 * half + 8 * n
                out_ref[start : start + 8, :] = slab_ref[
                    64 * n + 8 * dest : 64 * n + 8 * dest + 8, lanes
                ]
        out_ref[base + 32 : base + 40, :] = partial[0:8, :]


def pick_kernel(
    recv_ref, idx_ref, small_ref, inv_hbm, out_ref, table_ref, pick_ref, inv_ref, mid_ref,
    lift_ref, flip_ref, high_ref, low_ref, sem,
):
    copy = pltpu.make_async_copy(inv_hbm, inv_ref, sem)
    copy.start()
    sources = recv_ref.shape[0] // SLAB_ROWS

    def block_of(src, start):
        return recv_ref[pl.ds(SLAB_ROWS * src + start, 8), :]

    coarse = block_of(0, 32)
    for src in range(1, sources):
        coarse = coarse + block_of(src, 32)

    def build(p, carry):
        for half in range(2):
            start = pl.multiple_of(p * 48 + half * 24, 8)
            table_ref[pl.ds(start, 8), :] = block_of(2 * p, 16 * half)
            table_ref[pl.ds(start + 8, 8), :] = block_of(2 * p, 16 * half + 8) + block_of(
                2 * p + 1, 16 * half + 8
            )
            table_ref[pl.ds(start + 16, 8), :] = block_of(2 * p + 1, 16 * half)
        return carry

    lax.fori_loop(0, sources // 2, build, 0)
    gather_mixed(idx_ref, table_ref, pick_ref, flip_ref, high_ref, low_ref, 7, 72)
    mid_ref[...] = coarse
    copy.wait()
    coarse_rows = [jnp.broadcast_to(mid_ref[q : q + 1, :], (LANES, LANES)) for q in range(8)]
    ones = jnp.ones((16, LANES), BF16)
    for part in range(8):
        rows = slice(part * LANES, (part + 1) * LANES)
        product = inv_ref[rows, 0:LANES] * coarse_rows[0]
        for q in range(1, 8):
            product = product + inv_ref[rows, q * LANES : (q + 1) * LANES] * coarse_rows[q]
        high, low = split_pair(product)
        lift_ref[part : part + 1, :] = (pair_dot(ones, high) + pair_dot(ones, low))[0:1]
    lift = lift_ref[...]
    mine = own_lanes() == lax.rem(lax.axis_index("group"), 4)
    extra = jnp.where(mine, small_ref[0:2, :], 0.0)
    for h in range(pick_ref.shape[0] // 4):
        start = OWNER_ROWS * h
        out_ref[start : start + 8, :] = lift
        out_ref[start + 8 : start + 12, :] = pick_ref[4 * h : 4 * h + 4, :]
        out_ref[start + 12 : start + 14, :] = extra


def image_kernel(
    own_ref, pair_ref, dir_hbm, res_hbm, scale_hbm, iterate_hbm,
    image_ref, sums_ref, dir_ref, res_ref, scale_ref, iterate_ref,
    lift_ref, high_ref, low_ref, piece_ref, corr_ref, table_ref, flip_ref, pick_ref, wide_high_ref,
    wide_low_ref, sems,
):
    copies = start_copies(
        [
            (dir_hbm, dir_ref),
            (res_hbm, res_ref),
            (scale_hbm, scale_ref),
            (iterate_hbm, iterate_ref),
        ],
        sems,
    )
    groups = own_ref.shape[0] // OWNER_ROWS
    total = own_ref[0:8, :]
    for h in range(1, groups):
        total = total + own_ref[OWNER_ROWS * h : OWNER_ROWS * h + 8, :]
    lift_ref[...] = total

    def packed(row):
        rows = []
        for q in range(8):
            start = OWNER_ROWS * 4 * q + row
            value = own_ref[start : start + 1, :]
            for k in range(1, 4):
                start = OWNER_ROWS * (4 * q + k) + row
                value = value + own_ref[start : start + 1, :]
            rows.append(value)
        return jnp.concatenate(rows, axis=0).astype(jnp.int32)

    local = packed(12) - 512 * lax.axis_index("group")
    ids = packed(13)
    sender = 4 * lax.broadcasted_iota(jnp.int32, (8, LANES), 0) + jnp.broadcast_to(
        own_lanes(), (8, LANES)
    )
    valid = jnp.logical_and(local >= 0, local < 512)
    store_digits(jnp.where(valid, sender * 512 + local, -1), high_ref, low_ref)

    lifted = gather_rows(ids, lambda a: lift_ref[a : a + 1, :], 8)
    for n, piece in enumerate(split_channels(lifted, 3)):
        piece_ref[n] = piece
    corr_ref[...] = scatter_small(4 * groups, high_ref, low_ref, piece_ref, 8)
    for h in range(groups):
        start = OWNER_ROWS * h + 8
        table_ref[4 * h : 4 * h + 4, :] = (
            own_ref[start : start + 4, :] + corr_ref[4 * h : 4 * h + 4, :]
        )
    gather_mixed(pair_ref, table_ref, pick_ref, flip_ref, wide_high_ref, wide_low_ref, 4, 32)
    for copy in copies:
        copy.wait()
    half = dir_ref.shape[0]
    sums = [jnp.zeros((8, LANES), F32) for _ in range(4)]
    for start in range(0, half, 8):
        rows = slice(start, start + 8)
        image = pick_ref[rows, :] - pick_ref[half + start : half + start + 8, :]
        image_ref[rows, :] = image
        scaled = scale_ref[rows, :]
        scaled_res = res_ref[rows, :] * scaled
        sums[0] = sums[0] + scaled_res * res_ref[rows, :]
        sums[1] = sums[1] + dir_ref[rows, :] * image
        sums[2] = sums[2] + scaled_res * image
        sums[3] = sums[3] + (scaled * image) * image
    lane = lax.broadcasted_iota(jnp.int32, (8, LANES), 1)
    packed_sums = jnp.zeros((8, LANES), F32)
    for n, part in enumerate(sums):
        value = jnp.sum(jnp.sum(part, axis=0, keepdims=True), axis=1, keepdims=True)
        packed_sums = jnp.where(lane == n, jnp.broadcast_to(value, (8, LANES)), packed_sums)
    for t in range(sums_ref.shape[0] // 8):
        sums_ref[8 * t : 8 * t + 8, :] = packed_sums


def update_kernel(
    sums_ref, dir_ref, res_ref, scale_ref, iterate_ref, image_ref, it_out, res_out, dir_out
):
    totals = jnp.sum(sums_ref[...], axis=0, keepdims=True)
    lane = lax.broadcasted_iota(jnp.int32, (1, LANES), 1)

    def pick(n):
        return jnp.sum(jnp.where(lane == n, totals, 0.0), axis=1, keepdims=True)

    old, curvature, cross, square = pick(0), pick(1), pick(2), pick(3)
    alpha = old / curvature
    new = old - 2.0 * alpha * cross + (alpha * alpha) * square
    beta = new / old
    direction = dir_ref[...]
    res_next = res_ref[...] - alpha * image_ref[...]
    it_out[...] = iterate_ref[...] + alpha * direction
    res_out[...] = res_next
    dir_out[...] = scale_ref[...] * res_next + beta * direction


def exchange(array, axis):
    return lax.all_to_all(array, axis, split_axis=0, concat_axis=0, tiled=True)


def f32(*shape):
    return jax.ShapeDtypeStruct(shape, F32)


def i32(*shape):
    return jax.ShapeDtypeStruct(shape, jnp.int32)


def body(
    mult_iterate,
    residual,
    direction,
    mult_scale,
    eigen_basis,
    eigen_values,
    elastic_coef,
    coarse_inverse,
    send_pos,
    pair_slots,
    prim_rows,
    coarse_idx,
):
    groups = lax.axis_size("group")
    pencils = lax.axis_size("pencil")
    iterate_now = mult_iterate.reshape(64, LANES)
    resid_now = residual.reshape(64, LANES)
    search_dir = direction.reshape(64, LANES)
    scale_now = mult_scale.reshape(64, LANES)
    cells = send_pos.reshape(128, LANES)
    pairs = pair_slots.reshape(2, 8192)
    primal = prim_rows.reshape(1, 32)
    coarse_ids = coarse_idx.reshape(1, 32)

    def resident(array):
        return pltpu.with_memory_space_constraint(array, pltpu.HBM)

    digits = [pltpu.VMEM((128, LANES), F32), pltpu.VMEM((128, LANES), F32)]
    pieces = pltpu.VMEM((2, 128, LANES), F32)
    small = [
        pltpu.VMEM((8, LANES), F32),
        pltpu.VMEM((8, LANES), F32),
        pltpu.VMEM((3, 8, LANES), F32),
    ]
    sources = (
        pairs,
        search_dir,
        cells,
        primal,
        coarse_ids,
        eigen_basis,
        eigen_values.transpose(1, 0, 2),
        elastic_coef.transpose(1, 0, 2),
    )
    back, pair_rows, cells, primals, *patch_data = call(
        back_kernel,
        (
            f32(128, LANES),
            i32(128, LANES),
            i32(128, LANES),
            f32(8, LANES),
            f32(3, 64, 64),
            f32(3, 4, 64),
            f32(3, 4, 3),
        ),
        [HBM] * len(sources),
        "back",
        [
            pltpu.VMEM((2, 8192), jnp.int32),
            pltpu.VMEM((64, LANES), F32),
            pltpu.VMEM((1, 32), jnp.int32),
            pltpu.VMEM((1, 32), jnp.int32),
        ]
        + digits
        + [pieces, pltpu.VMEM((WIDE, LANES), F32), pltpu.SemaphoreType.DMA((len(sources),))],
    )(*(resident(source) for source in sources))
    arrived = exchange(back.reshape(groups, 4, LANES), "group").reshape(128, LANES)

    loads, slots = call(
        load_kernel,
        (f32(pencils * LOAD_ROWS, LANES), i32(128, LANES)),
        [VMEM] * 3,
        "load",
        digits + [pieces, pltpu.VMEM((192, LANES), F32)],
    )(arrived, cells, primals)
    columns = exchange(loads.reshape(pencils, 1, LOAD_ROWS * LANES), "pencil")

    partial = call(
        solve_kernel,
        f32(pencils * SLAB_ROWS, LANES),
        [VMEM] * 4,
        "solve",
        [
            pltpu.VMEM((128, 384), BF16),
            pltpu.VMEM((128, 384), BF16),
            pltpu.VMEM((256, 768), BF16),
            pltpu.VMEM((256, 768), BF16),
            pltpu.VMEM((6, 64, LANES), F32),
            pltpu.VMEM((256, LANES), F32),
            pltpu.VMEM((64, 8, LANES), F32),
            pltpu.VMEM((64, 8, LANES), F32),
            pltpu.VMEM((128, 256), F32),
        ]
        + small,
    )(columns.reshape(pencils * LOAD_ROWS, LANES), *patch_data)
    slabs = exchange(partial.reshape(pencils, 1, SLAB_ROWS * LANES), "pencil")

    picked = call(
        pick_kernel,
        f32(groups * OWNER_ROWS, LANES),
        [VMEM, VMEM, VMEM, HBM],
        "pick",
        [
            pltpu.VMEM((192, LANES), F32),
            pltpu.VMEM((128, LANES), F32),
            pltpu.VMEM((1024, 1024), F32),
            pltpu.VMEM((8, LANES), F32),
            pltpu.VMEM((8, LANES), F32),
            pltpu.VMEM((LANES, 384), BF16),
        ]
        + digits
        + [
            pltpu.SemaphoreType.DMA,
        ],
    )(slabs.reshape(pencils * SLAB_ROWS, LANES), slots, primals, resident(coarse_inverse))
    owner = exchange(picked.reshape(groups, 1, OWNER_ROWS * LANES), "group")

    shape = f32(64, LANES)
    image, sums, *vectors = call(
        image_kernel,
        (shape, f32(groups * pencils, LANES), shape, shape, shape, shape),
        [VMEM, VMEM] + [HBM] * 4,
        "image",
        [pltpu.VMEM((8, LANES), F32)]
        + small
        + [
            pltpu.VMEM((128, LANES), F32),
            pltpu.VMEM((128, LANES), F32),
            pltpu.VMEM((LANES, 256), BF16),
            pltpu.VMEM((128, LANES), F32),
        ]
        + digits
        + [pltpu.SemaphoreType.DMA((4,))],
    )(
        owner.reshape(groups * OWNER_ROWS, LANES),
        pair_rows,
        *(resident(array) for array in (search_dir, resid_now, scale_now, iterate_now)),
    )
    totals = exchange(sums, ("group", "pencil"))

    outs = call(update_kernel, (shape, shape, shape), [VMEM] * 6, "update")(
        totals, *vectors, image
    )
    return tuple(out.reshape(1, 1, -1) for out in outs)


def solution(mesh):
    in_specs = (
        P("group", "pencil", None),
        P("group", "pencil", None),
        P("group", "pencil", None),
        P("group", "pencil", None),
        P("group", None, None, None),
        P("group", None, None),
        P("group", None, None),
        P(),
        P("group", "pencil", None),
        P("group", "pencil", None, None),
        P("group", "pencil", None),
        P("group", "pencil", None),
    )
    out_specs = (P("group", "pencil", None), P("group", "pencil", None), P("group", "pencil", None))
    return jax.shard_map(body, mesh=mesh, in_specs=in_specs, out_specs=out_specs, check_vma=False)
```

```python
import jax
import jax.numpy as jnp
from jax import lax
from jax.experimental import pallas as pl
from jax.experimental.pallas import tpu as pltpu
from jax.sharding import PartitionSpec as P

LANES = 128
BF16 = jnp.bfloat16
F32 = jnp.float32
VMEM = pl.BlockSpec(memory_space=pltpu.VMEM)


HBM = pl.BlockSpec(memory_space=pltpu.HBM)


def call(kernel, out_shape, in_specs, name, scratch=(), flops=4_000_000):
    single = not isinstance(out_shape, (tuple, list))
    return pl.pallas_call(
        kernel,
        out_shape=out_shape,
        in_specs=in_specs,
        out_specs=VMEM if single else [VMEM] * len(out_shape),
        scratch_shapes=list(scratch),
        name=name,
        compiler_params=pltpu.CompilerParams(vmem_limit_bytes=16 << 20),
        cost_estimate=pl.CostEstimate(flops=flops, bytes_accessed=1 << 18, transcendentals=0),
    )


def split_channels(value, count):
    pieces = []
    for _ in range(count):
        piece = value.astype(BF16).astype(F32)
        pieces.append(piece)
        value = value - piece
    return pieces


def one_hot_parts(rows, high_row, low_row, piece_rows, chunk, channels):
    row_ids = lax.broadcasted_iota(jnp.int32, (rows, LANES), 0).astype(F32).astype(BF16)
    lane_ids = lax.broadcasted_iota(jnp.int32, (LANES, LANES), 0).astype(F32).astype(BF16)
    left, right = [], []
    for r in range(chunk):
        high = jnp.broadcast_to(high_row(r), (rows, LANES)).astype(BF16)
        low = jnp.broadcast_to(low_row(r), (LANES, LANES)).astype(BF16)
        left.append(jnp.where(row_ids == high, BF16(1), BF16(0)))
        match = lane_ids == low
        pieces = [
            jnp.where(
                match, jnp.broadcast_to(piece_rows(n, r), (LANES, LANES)).astype(BF16), BF16(0)
            )
            for n in range(channels)
        ]
        right.append(jnp.concatenate(pieces, axis=0))
    return jnp.concatenate(left, axis=1), jnp.concatenate(right, axis=1)


def pair_dot(left, right):
    return lax.dot_general(left, right, (((1,), (1,)), ((), ())), preferred_element_type=F32)


def scatter_large(rows, high_ref, low_ref, piece_row, total, chunk):
    def step(index, acc):
        left, right = one_hot_parts(
            rows,
            lambda r: high_ref[pl.ds(index * chunk + r, 1), :],
            lambda r: low_ref[pl.ds(index * chunk + r, 1), :],
            lambda n, r: piece_row(n, index, r),
            chunk,
            2,
        )
        return acc + pair_dot(right, left)

    acc = jnp.zeros((2 * LANES, rows), F32)
    if total == chunk:
        acc = step(0, acc)
    else:
        acc = lax.fori_loop(0, total // chunk, step, acc)
    return (acc[:LANES] + acc[LANES:]).T


def scatter_small(rows, high_ref, low_ref, piece_ref, count):
    left, right = one_hot_parts(
        rows,
        lambda r: high_ref[r : r + 1, :],
        lambda r: low_ref[r : r + 1, :],
        lambda n, r: piece_ref[n, r : r + 1, :],
        count,
        3,
    )
    acc = pair_dot(left, right)
    return acc[:, :LANES] + acc[:, LANES : 2 * LANES] + acc[:, 2 * LANES :]


def gather_rows(indices, table_row, table_rows):
    high = lax.shift_right_arithmetic(indices, 7)
    low = jnp.bitwise_and(indices, LANES - 1)
    acc = [jnp.zeros(indices.shape, F32) for _ in range(2)]
    for a in range(table_rows):
        row = jnp.broadcast_to(table_row(a), indices.shape)
        picked = jnp.take_along_axis(row, low, axis=1, mode="promise_in_bounds")
        acc[a % 2] = jnp.where(high == a, picked, acc[a % 2])
    return acc[0] + acc[1]


def gather_mixed(idx_ref, table_ref, out_ref, flip_ref, high_ref, low_ref, permuted, matched):
    table_rows = table_ref.shape[0]
    flipped = table_ref[...].T
    flip_ref[...] = jnp.concatenate(split_pair(flipped), axis=1)
    store_digits(idx_ref[...], high_ref, low_ref)
    row_ids = lax.broadcasted_iota(jnp.int32, (table_rows, LANES), 0).astype(F32).astype(BF16)
    lane_ids = lax.broadcasted_iota(jnp.int32, (LANES, LANES), 0).astype(F32)
    step = permuted * 8 + matched

    def block(t, carry):
        base = t * step
        second = base + permuted * 8
        select = []
        for r in range(matched):
            high = jnp.broadcast_to(high_ref[pl.ds(second + r, 1), :], (table_rows, LANES))
            select.append(jnp.where(row_ids == high.astype(BF16), BF16(1), BF16(0)))
        select = jnp.concatenate(select, axis=1)
        for sub in range(permuted):
            start = pl.multiple_of(base + 8 * sub, 8)
            out_ref[pl.ds(start, 8), :] = gather_rows(
                idx_ref[pl.ds(start, 8), :], lambda a: table_ref[a : a + 1, :], table_rows
            )
        rows = lax.dot_general(
            flip_ref[...],
            jnp.concatenate([select, select], axis=0),
            (((1,), (0,)), ((), ())),
            preferred_element_type=F32,
        )
        picked = []
        for r in range(matched):
            low = jnp.broadcast_to(low_ref[pl.ds(second + r, 1), :], (LANES, LANES))
            own = jnp.where(lane_ids == low, rows[:, r * LANES : (r + 1) * LANES], 0.0)
            picked.append(jnp.sum(own, axis=0, keepdims=True))
        out_ref[pl.ds(pl.multiple_of(second, 8), matched), :] = jnp.concatenate(picked, axis=0)
        return carry

    lax.fori_loop(0, idx_ref.shape[0] // step, block, 0)


def store_digits(idx, high_ref, low_ref):
    high_ref[...] = lax.shift_right_arithmetic(idx, 7).astype(F32)
    low_ref[...] = jnp.bitwise_and(idx, LANES - 1).astype(F32)


def floor_div(value, divisor):
    return jnp.floor((value + 0.5) * (1.0 / divisor))


def cell_digits(cells):
    cells = cells.astype(F32)
    plane = floor_div(cells, 252)
    spot = cells - 252.0 * plane
    slot = (
        spot
        + jnp.where(spot >= 64.0, 1.0, 0.0)
        + jnp.where(spot >= 126.0, 2.0, 0.0)
        + jnp.where(spot >= 188.0, 1.0, 0.0)
    )
    along_x = floor_div(plane, 12)
    rest = plane - 12.0 * along_x
    patch = floor_div(rest, 3)
    component = rest - 3.0 * patch
    half = jnp.where(slot >= 128.0, 1.0, 0.0)
    return patch, component, along_x, half, slot - 128.0 * half


def own_lanes():
    lane = lax.broadcasted_iota(jnp.int32, (1, LANES), 1)
    return lax.shift_right_logical(lane, 5)


def spread_lanes(row):
    return jnp.concatenate([row] * 4, axis=1)


CHUNK = 128
WIDE = 192
LOAD_ROWS = 34
SLAB_ROWS = 40
OWNER_ROWS = 14


def start_copies(pairs, sems):
    copies = [
        pltpu.make_async_copy(source, target, sems.at[n])
        for n, (source, target) in enumerate(pairs)
    ]
    for copy in copies:
        copy.start()
    return copies


def back_kernel(
    pair_hbm, dir_hbm, cells_hbm, prim_hbm, ids_hbm, basis_hbm, values_hbm, coeff_hbm,
    out_ref, idx_ref, cells_ref, small_ref, basis_ref, values_ref, coeff_ref,
    pair_ref, dir_ref, prim_ref, ids_ref,
    high_ref, low_ref, piece_ref, acc_ref, sems,
):
    patch = lax.div(lax.axis_index("pencil"), 2)
    copies = start_copies(
        [
            (pair_hbm, pair_ref),
            (dir_hbm, dir_ref),
            (cells_hbm, cells_ref),
            (prim_hbm, prim_ref),
            (ids_hbm, ids_ref),
            (basis_hbm.at[patch], basis_ref),
            (values_hbm, values_ref),
            (coeff_hbm, coeff_ref),
        ],
        sems,
    )
    half = dir_ref.shape[0]
    copies[0].wait()
    copies[1].wait()
    for k in range(half):
        both = pair_ref[:, k * LANES : (k + 1) * LANES]
        idx_ref[k : k + 1, :] = both[0:1]
        idx_ref[half + k : half + k + 1, :] = both[1:2]
    store_digits(idx_ref[...], high_ref, low_ref)
    for n, piece in enumerate(split_channels(dir_ref[...], 2)):
        piece_ref[n, :half, :] = piece
        piece_ref[n, half:, :] = -piece
    acc_ref[...] = scatter_large(
        WIDE,
        high_ref,
        low_ref,
        lambda n, t, r: piece_ref[n, pl.ds(t * CHUNK + r, 1), :],
        2 * half,
        CHUNK,
    )
    out_ref[...] = acc_ref[: 2 * half, :]
    for copy in copies[2:]:
        copy.wait()
    small_ref[...] = jnp.zeros(small_ref.shape, F32)
    small_ref[0:1, :] = spread_lanes(prim_ref[...].astype(F32))
    small_ref[1:2, :] = spread_lanes(ids_ref[...].astype(F32))


def load_kernel(
    arr_ref, pos_ref, small_ref, out_ref, slots_ref, high_ref, low_ref, piece_ref, acc_ref
):
    patch, component, along_x, half, lane = cell_digits(pos_ref[...])
    row = patch * 48.0 + half * 24.0 + component * 8.0 + along_x
    high_ref[...] = row
    low_ref[...] = lane
    slots_ref[...] = (row * 128.0 + lane).astype(jnp.int32)
    rows = pos_ref.shape[0]
    for n, piece in enumerate(split_channels(arr_ref[...], 2)):
        piece_ref[n] = piece
    acc_ref[...] = scatter_large(
        acc_ref.shape[0],
        high_ref,
        low_ref,
        lambda n, t, r: piece_ref[n, pl.ds(t * CHUNK + r, 1), :],
        rows,
        CHUNK,
    )
    pencil = lax.axis_index("pencil")
    mine = own_lanes() == lax.rem(pencil, 4)
    primal = jnp.broadcast_to(small_ref[0:1, :], (8, LANES)).astype(jnp.int32)
    cells = gather_rows(primal, lambda a: pos_ref[a : a + 1, :].astype(F32), rows)
    patch, component, along_x, half, lane = cell_digits(cells[0:1])
    place = half * 128.0 + along_x + (8 * pencil).astype(F32)
    code = place * 128.0 + lane
    ids = jnp.where(mine, small_ref[1:2, :], 0.0)
    for dest in range(out_ref.shape[0] // LOAD_ROWS):
        base = LOAD_ROWS * dest
        own = 2 * (dest % 2)
        for side in range(2):
            start = (dest // 2) * 48 + side * 24
            for n, c in enumerate((own, 1)):
                out_ref[base + side * 16 + 8 * n : base + side * 16 + 8 * n + 8, :] = acc_ref[
                    start + 8 * c : start + 8 * c + 8, :
                ]
        here = jnp.where(
            component == float(own), code, jnp.where(component == 1.0, code + 8192.0, -1.0)
        )
        here = jnp.where(patch == float(dest // 2), here, -1.0)
        out_ref[base + 32 : base + 33, :] = jnp.where(mine, here, 0.0)
        out_ref[base + 33 : base + 34, :] = ids


def split_pair(value):
    high = value.astype(BF16)
    return high, (value - high.astype(F32)).astype(BF16)


def store_left(ref, width, blocks):
    for row, lane, block in blocks:
        high, low = split_pair(block)
        for n, piece in enumerate((high, high, low)):
            start = n * width + lane
            ref[row : row + block.shape[0], start : start + block.shape[1]] = piece


def diagonal(outer, inner):
    return [(64 * n, 64 * n, block) for n, block in enumerate((outer, inner, inner, outer))]


def split_dot(left_ref, right, contract_right):
    high, low = split_pair(right)
    return lax.dot_general(
        left_ref[...],
        jnp.concatenate([high, low, high], axis=contract_right),
        (((1,), (contract_right,)), ((), ())),
        preferred_element_type=F32,
    )


def column_of(row):
    count = row.shape[1]
    first = lax.broadcasted_iota(jnp.int32, (count, count), 0)
    second = lax.broadcasted_iota(jnp.int32, (count, count), 1)
    spread = jnp.broadcast_to(row, (count, count))
    return jnp.sum(jnp.where(first == second, spread, 0.0), axis=1, keepdims=True)


def solve_kernel(
    recv_ref, basis_ref, values_ref, coeff_ref, out_ref, bxt_ref, bx_ref, bdt_ref, bd_ref, cst_ref,
    fwd_ref, d0_ref, d1_ref, slab_ref, high_ref, low_ref, piece_ref,
):
    pencil = lax.axis_index("pencil")
    patch = lax.div(pencil, 2)
    side = lax.rem(pencil, 2)
    for ref in (bx_ref, bxt_ref, bd_ref, bdt_ref):
        ref[...] = jnp.zeros(ref.shape, BF16)
    along_x, along_y, along_z = basis_ref[0], basis_ref[1], basis_ref[2]
    half_x = jnp.where(side == 1, along_x[:, 32:64], along_x[:, 0:32])
    flipped = along_x.T
    half_flipped = jnp.where(side == 1, flipped[32:64], flipped[0:32])
    flipped_y = along_y.T
    flipped_z = along_z.T
    store_left(bx_ref, 128, [(0, 0, along_x), (64, 64, half_x)])
    store_left(bxt_ref, 128, [(0, 0, flipped), (64, 64, half_flipped)])
    store_left(bd_ref, 256, diagonal(along_z, along_y))
    store_left(bdt_ref, 256, diagonal(flipped_z, flipped_y))

    def spread(column):
        return jnp.broadcast_to(column, (64, LANES))

    cst_ref[0] = spread(column_of(along_y[0:1]))
    cst_ref[1] = spread(column_of(along_y[63:64]))
    cst_ref[2] = spread(column_of(along_z[0:1]))
    cst_ref[3] = spread(column_of(along_z[63:64]))
    lane = lax.broadcasted_iota(jnp.int32, (1, LANES), 1)

    def weight(dim):
        own = jnp.where(
            side == 1, coeff_ref[2, pl.ds(patch, 1), :], coeff_ref[0, pl.ds(patch, 1), :]
        )
        shared = coeff_ref[1, pl.ds(patch, 1), :]
        own, shared = (
            jnp.broadcast_to(value[:, dim : dim + 1], (1, LANES)) for value in (own, shared)
        )
        return jnp.where(lane < 64, own, jnp.where(lane < 96, shared, 0.0))

    x_values, y_values, z_values = (values_ref[dim, pl.ds(patch, 1), :] for dim in range(3))
    half_values = jnp.where(side == 1, x_values[:, 32:64], x_values[:, 0:32])
    lane_values = jnp.concatenate([x_values, half_values, half_values], axis=1)
    x_term = jnp.where(lane >= 96, 1.0, weight(0) * lane_values)
    y_term = weight(1) * spread(column_of(y_values))
    cst_ref[4] = x_term + y_term
    cst_ref[5] = weight(2) * spread(column_of(z_values))

    sources = recv_ref.shape[0] // LOAD_ROWS
    load = jnp.concatenate(
        [
            jnp.concatenate(
                [
                    recv_ref[LOAD_ROWS * src + start : LOAD_ROWS * src + start + 8, :]
                    for start in (8 * n, 16 + 8 * n)
                ],
                axis=1,
            )
            for n in range(2)
            for src in range(sources)
        ],
        axis=0,
    )
    fwd_ref[...] = split_dot(bdt_ref, split_dot(bxt_ref, load, 0), 1)

    def step(j, carry):
        top, bottom = carry

        def row(index):
            return jnp.broadcast_to(cst_ref[index, pl.ds(j, 1), :], (64, LANES))

        first = jnp.broadcast_to(fwd_ref[pl.ds(64 + j, 1), :], (64, LANES))
        last = jnp.broadcast_to(fwd_ref[pl.ds(128 + j, 1), :], (64, LANES))
        y_first, y_last = row(0), row(1)
        spectral = (
            y_first * fwd_ref[0:64, :]
            + y_last * fwd_ref[192:256, :]
            + first * cst_ref[2]
            + last * cst_ref[3]
        )
        scaled = spectral / (row(4) + cst_ref[5])
        along_first = cst_ref[2] * scaled
        along_last = cst_ref[3] * scaled
        d0_ref[j] = jnp.sum(along_first.reshape(8, 8, LANES), axis=0)
        d1_ref[j] = jnp.sum(along_last.reshape(8, 8, LANES), axis=0)
        return top + y_first * scaled, bottom + y_last * scaled

    zero = jnp.zeros((64, LANES), F32)
    top, bottom = lax.fori_loop(0, 64, step, (zero, zero), unroll=8)
    edges = jnp.concatenate(
        [top, jnp.sum(d0_ref[...], axis=1), jnp.sum(d1_ref[...], axis=1), bottom], axis=0
    )
    slab_ref[...] = split_dot(bx_ref, split_dot(bd_ref, edges, 0), 1)

    def packed(row):
        halves = []
        for part in range(2):
            starts = [LOAD_ROWS * (4 * part + k) + row for k in range(4)]
            value = recv_ref[starts[0] : starts[0] + 1, :]
            for start in starts[1:]:
                value = value + recv_ref[start : start + 1, :]
            halves.append(value)
        return jnp.concatenate(halves + [jnp.full((6, LANES), -1.0, F32)], axis=0)

    codes = packed(32).astype(jnp.int32)
    ids = packed(33).astype(jnp.int32)
    primal = gather_rows(
        codes,
        lambda a: slab_ref[a % 128 : a % 128 + 1, (a // 128) * LANES : (a // 128 + 1) * LANES],
        256,
    )
    store_digits(ids, high_ref, low_ref)
    for n, piece in enumerate(split_channels(primal, 3)):
        piece_ref[n] = piece
    partial = scatter_small(16, high_ref, low_ref, piece_ref, 2)
    for dest in range(out_ref.shape[0] // SLAB_ROWS):
        base = SLAB_ROWS * dest
        for half in range(2):
            lanes = slice(half * LANES, (half + 1) * LANES)
            for n in range(2):
                start = base + 16 * half + 8 * n
                out_ref[start : start + 8, :] = slab_ref[
                    64 * n + 8 * dest : 64 * n + 8 * dest + 8, lanes
                ]
        out_ref[base + 32 : base + 40, :] = partial[0:8, :]


def pick_kernel(
    recv_ref, idx_ref, small_ref, inv_hbm, out_ref, table_ref, pick_ref, inv_ref, mid_ref,
    lift_ref, flip_ref, high_ref, low_ref, sem,
):
    copy = pltpu.make_async_copy(inv_hbm, inv_ref, sem)
    copy.start()
    sources = recv_ref.shape[0] // SLAB_ROWS

    def block_of(src, start):
        return recv_ref[pl.ds(SLAB_ROWS * src + start, 8), :]

    coarse = block_of(0, 32)
    for src in range(1, sources):
        coarse = coarse + block_of(src, 32)

    def build(p, carry):
        for half in range(2):
            start = pl.multiple_of(p * 48 + half * 24, 8)
            table_ref[pl.ds(start, 8), :] = block_of(2 * p, 16 * half)
            table_ref[pl.ds(start + 8, 8), :] = block_of(2 * p, 16 * half + 8) + block_of(
                2 * p + 1, 16 * half + 8
            )
            table_ref[pl.ds(start + 16, 8), :] = block_of(2 * p + 1, 16 * half)
        return carry

    lax.fori_loop(0, sources // 2, build, 0)
    gather_mixed(idx_ref, table_ref, pick_ref, flip_ref, high_ref, low_ref, 7, 72)
    mid_ref[...] = coarse
    copy.wait()
    coarse_rows = [jnp.broadcast_to(mid_ref[q : q + 1, :], (LANES, LANES)) for q in range(8)]
    ones = jnp.ones((16, LANES), BF16)
    for part in range(8):
        rows = slice(part * LANES, (part + 1) * LANES)
        product = inv_ref[rows, 0:LANES] * coarse_rows[0]
        for q in range(1, 8):
            product = product + inv_ref[rows, q * LANES : (q + 1) * LANES] * coarse_rows[q]
        high, low = split_pair(product)
        lift_ref[part : part + 1, :] = (pair_dot(ones, high) + pair_dot(ones, low))[0:1]
    lift = lift_ref[...]
    mine = own_lanes() == lax.rem(lax.axis_index("group"), 4)
    extra = jnp.where(mine, small_ref[0:2, :], 0.0)
    for h in range(pick_ref.shape[0] // 4):
        start = OWNER_ROWS * h
        out_ref[start : start + 8, :] = lift
        out_ref[start + 8 : start + 12, :] = pick_ref[4 * h : 4 * h + 4, :]
        out_ref[start + 12 : start + 14, :] = extra


def image_kernel(
    own_ref, pair_ref, dir_hbm, res_hbm, scale_hbm, iterate_hbm,
    image_ref, sums_ref, dir_ref, res_ref, scale_ref, iterate_ref,
    lift_ref, high_ref, low_ref, piece_ref, corr_ref, table_ref, flip_ref, pick_ref, wide_high_ref,
    wide_low_ref, sems,
):
    copies = start_copies(
        [
            (dir_hbm, dir_ref),
            (res_hbm, res_ref),
            (scale_hbm, scale_ref),
            (iterate_hbm, iterate_ref),
        ],
        sems,
    )
    groups = own_ref.shape[0] // OWNER_ROWS
    total = own_ref[0:8, :]
    for h in range(1, groups):
        total = total + own_ref[OWNER_ROWS * h : OWNER_ROWS * h + 8, :]
    lift_ref[...] = total

    def packed(row):
        rows = []
        for q in range(8):
            start = OWNER_ROWS * 4 * q + row
            value = own_ref[start : start + 1, :]
            for k in range(1, 4):
                start = OWNER_ROWS * (4 * q + k) + row
                value = value + own_ref[start : start + 1, :]
            rows.append(value)
        return jnp.concatenate(rows, axis=0).astype(jnp.int32)

    local = packed(12) - 512 * lax.axis_index("group")
    ids = packed(13)
    sender = 4 * lax.broadcasted_iota(jnp.int32, (8, LANES), 0) + jnp.broadcast_to(
        own_lanes(), (8, LANES)
    )
    valid = jnp.logical_and(local >= 0, local < 512)
    store_digits(jnp.where(valid, sender * 512 + local, -1), high_ref, low_ref)

    lifted = gather_rows(ids, lambda a: lift_ref[a : a + 1, :], 8)
    for n, piece in enumerate(split_channels(lifted, 3)):
        piece_ref[n] = piece
    corr_ref[...] = scatter_small(4 * groups, high_ref, low_ref, piece_ref, 8)
    for h in range(groups):
        start = OWNER_ROWS * h + 8
        table_ref[4 * h : 4 * h + 4, :] = (
            own_ref[start : start + 4, :] + corr_ref[4 * h : 4 * h + 4, :]
        )
    gather_mixed(pair_ref, table_ref, pick_ref, flip_ref, wide_high_ref, wide_low_ref, 4, 32)
    for copy in copies:
        copy.wait()
    half = dir_ref.shape[0]
    sums = [jnp.zeros((8, LANES), F32) for _ in range(4)]
    for start in range(0, half, 8):
        rows = slice(start, start + 8)
        image = pick_ref[rows, :] - pick_ref[half + start : half + start + 8, :]
        image_ref[rows, :] = image
        scaled = scale_ref[rows, :]
        scaled_res = res_ref[rows, :] * scaled
        sums[0] = sums[0] + scaled_res * res_ref[rows, :]
        sums[1] = sums[1] + dir_ref[rows, :] * image
        sums[2] = sums[2] + scaled_res * image
        sums[3] = sums[3] + (scaled * image) * image
    lane = lax.broadcasted_iota(jnp.int32, (8, LANES), 1)
    packed_sums = jnp.zeros((8, LANES), F32)
    for n, part in enumerate(sums):
        value = jnp.sum(jnp.sum(part, axis=0, keepdims=True), axis=1, keepdims=True)
        packed_sums = jnp.where(lane == n, jnp.broadcast_to(value, (8, LANES)), packed_sums)
    for t in range(sums_ref.shape[0] // 8):
        sums_ref[8 * t : 8 * t + 8, :] = packed_sums


def update_kernel(
    sums_ref, dir_ref, res_ref, scale_ref, iterate_ref, image_ref, it_out, res_out, dir_out
):
    totals = jnp.sum(sums_ref[...], axis=0, keepdims=True)
    lane = lax.broadcasted_iota(jnp.int32, (1, LANES), 1)

    def pick(n):
        return jnp.sum(jnp.where(lane == n, totals, 0.0), axis=1, keepdims=True)

    old, curvature, cross, square = pick(0), pick(1), pick(2), pick(3)
    alpha = old / curvature
    new = old - 2.0 * alpha * cross + (alpha * alpha) * square
    beta = new / old
    direction = dir_ref[...]
    res_next = res_ref[...] - alpha * image_ref[...]
    it_out[...] = iterate_ref[...] + alpha * direction
    res_out[...] = res_next
    dir_out[...] = scale_ref[...] * res_next + beta * direction


def exchange(array, axis):
    return lax.all_to_all(array, axis, split_axis=0, concat_axis=0, tiled=True)


def f32(*shape):
    return jax.ShapeDtypeStruct(shape, F32)


def i32(*shape):
    return jax.ShapeDtypeStruct(shape, jnp.int32)


def body(
    mult_iterate,
    residual,
    direction,
    mult_scale,
    eigen_basis,
    eigen_values,
    elastic_coef,
    coarse_inverse,
    send_pos,
    pair_slots,
    prim_rows,
    coarse_idx,
):
    groups = lax.axis_size("group")
    pencils = lax.axis_size("pencil")
    iterate_now = mult_iterate.reshape(64, LANES)
    resid_now = residual.reshape(64, LANES)
    search_dir = direction.reshape(64, LANES)
    scale_now = mult_scale.reshape(64, LANES)
    cells = send_pos.reshape(128, LANES)
    pairs = pair_slots.reshape(2, 8192)
    primal = prim_rows.reshape(1, 32)
    coarse_ids = coarse_idx.reshape(1, 32)

    def resident(array):
        return pltpu.with_memory_space_constraint(array, pltpu.HBM)

    digits = [pltpu.VMEM((128, LANES), F32), pltpu.VMEM((128, LANES), F32)]
    pieces = pltpu.VMEM((2, 128, LANES), F32)
    small = [
        pltpu.VMEM((8, LANES), F32),
        pltpu.VMEM((8, LANES), F32),
        pltpu.VMEM((3, 8, LANES), F32),
    ]
    sources = (
        pairs,
        search_dir,
        cells,
        primal,
        coarse_ids,
        eigen_basis,
        eigen_values.transpose(1, 0, 2),
        elastic_coef.transpose(1, 0, 2),
    )
    back, pair_rows, cells, primals, *patch_data = call(
        back_kernel,
        (
            f32(128, LANES),
            i32(128, LANES),
            i32(128, LANES),
            f32(8, LANES),
            f32(3, 64, 64),
            f32(3, 4, 64),
            f32(3, 4, 3),
        ),
        [HBM] * len(sources),
        "back",
        [
            pltpu.VMEM((2, 8192), jnp.int32),
            pltpu.VMEM((64, LANES), F32),
            pltpu.VMEM((1, 32), jnp.int32),
            pltpu.VMEM((1, 32), jnp.int32),
        ]
        + digits
        + [pieces, pltpu.VMEM((WIDE, LANES), F32), pltpu.SemaphoreType.DMA((len(sources),))],
    )(*(resident(source) for source in sources))
    arrived = exchange(back.reshape(groups, 4, LANES), "group").reshape(128, LANES)

    loads, slots = call(
        load_kernel,
        (f32(pencils * LOAD_ROWS, LANES), i32(128, LANES)),
        [VMEM] * 3,
        "load",
        digits + [pieces, pltpu.VMEM((192, LANES), F32)],
    )(arrived, cells, primals)
    columns = exchange(loads.reshape(pencils, 1, LOAD_ROWS * LANES), "pencil")

    partial = call(
        solve_kernel,
        f32(pencils * SLAB_ROWS, LANES),
        [VMEM] * 4,
        "solve",
        [
            pltpu.VMEM((128, 384), BF16),
            pltpu.VMEM((128, 384), BF16),
            pltpu.VMEM((256, 768), BF16),
            pltpu.VMEM((256, 768), BF16),
            pltpu.VMEM((6, 64, LANES), F32),
            pltpu.VMEM((256, LANES), F32),
            pltpu.VMEM((64, 8, LANES), F32),
            pltpu.VMEM((64, 8, LANES), F32),
            pltpu.VMEM((128, 256), F32),
        ]
        + small,
    )(columns.reshape(pencils * LOAD_ROWS, LANES), *patch_data)
    slabs = exchange(partial.reshape(pencils, 1, SLAB_ROWS * LANES), "pencil")

    picked = call(
        pick_kernel,
        f32(groups * OWNER_ROWS, LANES),
        [VMEM, VMEM, VMEM, HBM],
        "pick",
        [
            pltpu.VMEM((192, LANES), F32),
            pltpu.VMEM((128, LANES), F32),
            pltpu.VMEM((1024, 1024), F32),
            pltpu.VMEM((8, LANES), F32),
            pltpu.VMEM((8, LANES), F32),
            pltpu.VMEM((LANES, 384), BF16),
        ]
        + digits
        + [
            pltpu.SemaphoreType.DMA,
        ],
    )(slabs.reshape(pencils * SLAB_ROWS, LANES), slots, primals, resident(coarse_inverse))
    owner = exchange(picked.reshape(groups, 1, OWNER_ROWS * LANES), "group")

    shape = f32(64, LANES)
    image, sums, *vectors = call(
        image_kernel,
        (shape, f32(groups * pencils, LANES), shape, shape, shape, shape),
        [VMEM, VMEM] + [HBM] * 4,
        "image",
        [pltpu.VMEM((8, LANES), F32)]
        + small
        + [
            pltpu.VMEM((128, LANES), F32),
            pltpu.VMEM((128, LANES), F32),
            pltpu.VMEM((LANES, 256), BF16),
            pltpu.VMEM((128, LANES), F32),
        ]
        + digits
        + [pltpu.SemaphoreType.DMA((4,))],
    )(
        owner.reshape(groups * OWNER_ROWS, LANES),
        pair_rows,
        *(resident(array) for array in (search_dir, resid_now, scale_now, iterate_now)),
    )
    totals = exchange(sums, ("group", "pencil"))

    outs = call(update_kernel, (shape, shape, shape), [VMEM] * 6, "update")(
        totals, *vectors, image
    )
    return tuple(out.reshape(1, 1, -1) for out in outs)


def solution(mesh):
    in_specs = (
        P("group", "pencil", None),
        P("group", "pencil", None),
        P("group", "pencil", None),
        P("group", "pencil", None),
        P("group", None, None, None),
        P("group", None, None),
        P("group", None, None),
        P(),
        P("group", "pencil", None),
        P("group", "pencil", None, None),
        P("group", "pencil", None),
        P("group", "pencil", None),
    )
    out_specs = (P("group", "pencil", None), P("group", "pencil", None), P("group", "pencil", None))
    return jax.shard_map(body, mesh=mesh, in_specs=in_specs, out_specs=out_specs, check_vma=False)
```

```python
import jax
import jax.numpy as jnp
from jax import lax
from jax.experimental import pallas as pl
from jax.experimental.pallas import tpu as pltpu
from jax.sharding import PartitionSpec as P

LANES = 128
BF16 = jnp.bfloat16
F32 = jnp.float32
VMEM = pl.BlockSpec(memory_space=pltpu.VMEM)


HBM = pl.BlockSpec(memory_space=pltpu.HBM)


def call(kernel, out_shape, in_specs, name, scratch=(), flops=4_000_000):
    single = not isinstance(out_shape, (tuple, list))
    return pl.pallas_call(
        kernel,
        out_shape=out_shape,
        in_specs=in_specs,
        out_specs=VMEM if single else [VMEM] * len(out_shape),
        scratch_shapes=list(scratch),
        name=name,
        compiler_params=pltpu.CompilerParams(vmem_limit_bytes=16 << 20),
        cost_estimate=pl.CostEstimate(flops=flops, bytes_accessed=1 << 18, transcendentals=0),
    )


def split_channels(value, count):
    pieces = []
    for _ in range(count):
        piece = value.astype(BF16).astype(F32)
        pieces.append(piece)
        value = value - piece
    return pieces


def one_hot_parts(rows, high_row, low_row, piece_rows, chunk, channels):
    row_ids = lax.broadcasted_iota(jnp.int32, (rows, LANES), 0).astype(F32).astype(BF16)
    lane_ids = lax.broadcasted_iota(jnp.int32, (LANES, LANES), 0).astype(F32).astype(BF16)
    left, right = [], []
    for r in range(chunk):
        high = jnp.broadcast_to(high_row(r), (rows, LANES)).astype(BF16)
        low = jnp.broadcast_to(low_row(r), (LANES, LANES)).astype(BF16)
        left.append(jnp.where(row_ids == high, BF16(1), BF16(0)))
        match = lane_ids == low
        pieces = [
            jnp.where(
                match, jnp.broadcast_to(piece_rows(n, r), (LANES, LANES)).astype(BF16), BF16(0)
            )
            for n in range(channels)
        ]
        right.append(jnp.concatenate(pieces, axis=0))
    return jnp.concatenate(left, axis=1), jnp.concatenate(right, axis=1)


def pair_dot(left, right):
    return lax.dot_general(left, right, (((1,), (1,)), ((), ())), preferred_element_type=F32)


def scatter_large(rows, high_ref, low_ref, piece_row, total, chunk):
    def step(index, acc):
        left, right = one_hot_parts(
            rows,
            lambda r: high_ref[pl.ds(index * chunk + r, 1), :],
            lambda r: low_ref[pl.ds(index * chunk + r, 1), :],
            lambda n, r: piece_row(n, index, r),
            chunk,
            2,
        )
        return acc + pair_dot(right, left)

    acc = jnp.zeros((2 * LANES, rows), F32)
    if total == chunk:
        acc = step(0, acc)
    else:
        acc = lax.fori_loop(0, total // chunk, step, acc)
    return (acc[:LANES] + acc[LANES:]).T


def scatter_small(rows, high_ref, low_ref, piece_ref, count):
    left, right = one_hot_parts(
        rows,
        lambda r: high_ref[r : r + 1, :],
        lambda r: low_ref[r : r + 1, :],
        lambda n, r: piece_ref[n, r : r + 1, :],
        count,
        3,
    )
    acc = pair_dot(left, right)
    return acc[:, :LANES] + acc[:, LANES : 2 * LANES] + acc[:, 2 * LANES :]


def gather_rows(indices, table_row, table_rows):
    high = lax.shift_right_arithmetic(indices, 7)
    low = jnp.bitwise_and(indices, LANES - 1)
    acc = [jnp.zeros(indices.shape, F32) for _ in range(2)]
    for a in range(table_rows):
        row = jnp.broadcast_to(table_row(a), indices.shape)
        picked = jnp.take_along_axis(row, low, axis=1, mode="promise_in_bounds")
        acc[a % 2] = jnp.where(high == a, picked, acc[a % 2])
    return acc[0] + acc[1]


def gather_mixed(idx_ref, table_ref, out_ref, flip_ref, high_ref, low_ref, permuted, matched):
    table_rows = table_ref.shape[0]
    flipped = table_ref[...].T
    flip_ref[...] = jnp.concatenate(split_pair(flipped), axis=1)
    store_digits(idx_ref[...], high_ref, low_ref)
    row_ids = lax.broadcasted_iota(jnp.int32, (table_rows, LANES), 0).astype(F32).astype(BF16)
    lane_ids = lax.broadcasted_iota(jnp.int32, (LANES, LANES), 0).astype(F32)
    step = permuted * 8 + matched

    def block(t, carry):
        base = t * step
        second = base + permuted * 8
        select = []
        for r in range(matched):
            high = jnp.broadcast_to(high_ref[pl.ds(second + r, 1), :], (table_rows, LANES))
            select.append(jnp.where(row_ids == high.astype(BF16), BF16(1), BF16(0)))
        select = jnp.concatenate(select, axis=1)
        for sub in range(permuted):
            start = pl.multiple_of(base + 8 * sub, 8)
            out_ref[pl.ds(start, 8), :] = gather_rows(
                idx_ref[pl.ds(start, 8), :], lambda a: table_ref[a : a + 1, :], table_rows
            )
        rows = lax.dot_general(
            flip_ref[...],
            jnp.concatenate([select, select], axis=0),
            (((1,), (0,)), ((), ())),
            preferred_element_type=F32,
        )
        picked = []
        for r in range(matched):
            low = jnp.broadcast_to(low_ref[pl.ds(second + r, 1), :], (LANES, LANES))
            own = jnp.where(lane_ids == low, rows[:, r * LANES : (r + 1) * LANES], 0.0)
            picked.append(jnp.sum(own, axis=0, keepdims=True))
        out_ref[pl.ds(pl.multiple_of(second, 8), matched), :] = jnp.concatenate(picked, axis=0)
        return carry

    lax.fori_loop(0, idx_ref.shape[0] // step, block, 0)


def store_digits(idx, high_ref, low_ref):
    high_ref[...] = lax.shift_right_arithmetic(idx, 7).astype(F32)
    low_ref[...] = jnp.bitwise_and(idx, LANES - 1).astype(F32)


def floor_div(value, divisor):
    return jnp.floor((value + 0.5) * (1.0 / divisor))


def cell_digits(cells):
    cells = cells.astype(F32)
    plane = floor_div(cells, 252)
    spot = cells - 252.0 * plane
    slot = (
        spot
        + jnp.where(spot >= 64.0, 1.0, 0.0)
        + jnp.where(spot >= 126.0, 2.0, 0.0)
        + jnp.where(spot >= 188.0, 1.0, 0.0)
    )
    along_x = floor_div(plane, 12)
    rest = plane - 12.0 * along_x
    patch = floor_div(rest, 3)
    component = rest - 3.0 * patch
    half = jnp.where(slot >= 128.0, 1.0, 0.0)
    return patch, component, along_x, half, slot - 128.0 * half


def own_lanes():
    lane = lax.broadcasted_iota(jnp.int32, (1, LANES), 1)
    return lax.shift_right_logical(lane, 5)


def spread_lanes(row):
    return jnp.concatenate([row] * 4, axis=1)


CHUNK = 128
WIDE = 192
LOAD_ROWS = 34
SLAB_ROWS = 40
OWNER_ROWS = 14


def start_copies(pairs, sems):
    copies = [
        pltpu.make_async_copy(source, target, sems.at[n])
        for n, (source, target) in enumerate(pairs)
    ]
    for copy in copies:
        copy.start()
    return copies


def back_kernel(
    pair_hbm, dir_hbm, cells_hbm, prim_hbm, ids_hbm, basis_hbm, values_hbm, coeff_hbm,
    out_ref, idx_ref, cells_ref, small_ref, basis_ref, values_ref, coeff_ref,
    pair_ref, dir_ref, prim_ref, ids_ref,
    high_ref, low_ref, piece_ref, acc_ref, sems,
):
    patch = lax.div(lax.axis_index("pencil"), 2)
    copies = start_copies(
        [
            (pair_hbm, pair_ref),
            (dir_hbm, dir_ref),
            (cells_hbm, cells_ref),
            (prim_hbm, prim_ref),
            (ids_hbm, ids_ref),
            (basis_hbm.at[patch], basis_ref),
            (values_hbm, values_ref),
            (coeff_hbm, coeff_ref),
        ],
        sems,
    )
    half = dir_ref.shape[0]
    copies[0].wait()
    copies[1].wait()
    for k in range(half):
        both = pair_ref[:, k * LANES : (k + 1) * LANES]
        idx_ref[k : k + 1, :] = both[0:1]
        idx_ref[half + k : half + k + 1, :] = both[1:2]
    store_digits(idx_ref[...], high_ref, low_ref)
    for n, piece in enumerate(split_channels(dir_ref[...], 2)):
        piece_ref[n, :half, :] = piece
        piece_ref[n, half:, :] = -piece
    acc_ref[...] = scatter_large(
        WIDE,
        high_ref,
        low_ref,
        lambda n, t, r: piece_ref[n, pl.ds(t * CHUNK + r, 1), :],
        2 * half,
        CHUNK,
    )
    out_ref[...] = acc_ref[: 2 * half, :]
    for copy in copies[2:]:
        copy.wait()
    small_ref[...] = jnp.zeros(small_ref.shape, F32)
    small_ref[0:1, :] = spread_lanes(prim_ref[...].astype(F32))
    small_ref[1:2, :] = spread_lanes(ids_ref[...].astype(F32))


def load_kernel(
    arr_ref, pos_ref, small_ref, out_ref, slots_ref, high_ref, low_ref, piece_ref, acc_ref
):
    patch, component, along_x, half, lane = cell_digits(pos_ref[...])
    row = patch * 48.0 + half * 24.0 + component * 8.0 + along_x
    high_ref[...] = row
    low_ref[...] = lane
    slots_ref[...] = (row * 128.0 + lane).astype(jnp.int32)
    rows = pos_ref.shape[0]
    for n, piece in enumerate(split_channels(arr_ref[...], 2)):
        piece_ref[n] = piece
    acc_ref[...] = scatter_large(
        acc_ref.shape[0],
        high_ref,
        low_ref,
        lambda n, t, r: piece_ref[n, pl.ds(t * CHUNK + r, 1), :],
        rows,
        CHUNK,
    )
    pencil = lax.axis_index("pencil")
    mine = own_lanes() == lax.rem(pencil, 4)
    primal = jnp.broadcast_to(small_ref[0:1, :], (8, LANES)).astype(jnp.int32)
    cells = gather_rows(primal, lambda a: pos_ref[a : a + 1, :].astype(F32), rows)
    patch, component, along_x, half, lane = cell_digits(cells[0:1])
    place = half * 128.0 + along_x + (8 * pencil).astype(F32)
    code = place * 128.0 + lane
    ids = jnp.where(mine, small_ref[1:2, :], 0.0)
    for dest in range(out_ref.shape[0] // LOAD_ROWS):
        base = LOAD_ROWS * dest
        own = 2 * (dest % 2)
        for side in range(2):
            start = (dest // 2) * 48 + side * 24
            for n, c in enumerate((own, 1)):
                out_ref[base + side * 16 + 8 * n : base + side * 16 + 8 * n + 8, :] = acc_ref[
                    start + 8 * c : start + 8 * c + 8, :
                ]
        here = jnp.where(
            component == float(own), code, jnp.where(component == 1.0, code + 8192.0, -1.0)
        )
        here = jnp.where(patch == float(dest // 2), here, -1.0)
        out_ref[base + 32 : base + 33, :] = jnp.where(mine, here, 0.0)
        out_ref[base + 33 : base + 34, :] = ids


def split_pair(value):
    high = value.astype(BF16)
    return high, (value - high.astype(F32)).astype(BF16)


def store_left(ref, width, blocks):
    for row, lane, block in blocks:
        high, low = split_pair(block)
        for n, piece in enumerate((high, high, low)):
            start = n * width + lane
            ref[row : row + block.shape[0], start : start + block.shape[1]] = piece


def diagonal(outer, inner):
    return [(64 * n, 64 * n, block) for n, block in enumerate((outer, inner, inner, outer))]


def split_dot(left_ref, right, contract_right):
    high, low = split_pair(right)
    return lax.dot_general(
        left_ref[...],
        jnp.concatenate([high, low, high], axis=contract_right),
        (((1,), (contract_right,)), ((), ())),
        preferred_element_type=F32,
    )


def column_of(row):
    count = row.shape[1]
    first = lax.broadcasted_iota(jnp.int32, (count, count), 0)
    second = lax.broadcasted_iota(jnp.int32, (count, count), 1)
    spread = jnp.broadcast_to(row, (count, count))
    return jnp.sum(jnp.where(first == second, spread, 0.0), axis=1, keepdims=True)


def solve_kernel(
    recv_ref, basis_ref, values_ref, coeff_ref, out_ref, bxt_ref, bx_ref, bdt_ref, bd_ref, cst_ref,
    fwd_ref, d0_ref, d1_ref, slab_ref, high_ref, low_ref, piece_ref,
):
    pencil = lax.axis_index("pencil")
    patch = lax.div(pencil, 2)
    side = lax.rem(pencil, 2)
    for ref in (bx_ref, bxt_ref, bd_ref, bdt_ref):
        ref[...] = jnp.zeros(ref.shape, BF16)
    along_x, along_y, along_z = basis_ref[0], basis_ref[1], basis_ref[2]
    half_x = jnp.where(side == 1, along_x[:, 32:64], along_x[:, 0:32])
    flipped = along_x.T
    half_flipped = jnp.where(side == 1, flipped[32:64], flipped[0:32])
    flipped_y = along_y.T
    flipped_z = along_z.T
    store_left(bx_ref, 128, [(0, 0, along_x), (64, 64, half_x)])
    store_left(bxt_ref, 128, [(0, 0, flipped), (64, 64, half_flipped)])
    store_left(bd_ref, 256, diagonal(along_z, along_y))
    store_left(bdt_ref, 256, diagonal(flipped_z, flipped_y))

    def spread(column):
        return jnp.broadcast_to(column, (64, LANES))

    cst_ref[0] = spread(column_of(along_y[0:1]))
    cst_ref[1] = spread(column_of(along_y[63:64]))
    cst_ref[2] = spread(column_of(along_z[0:1]))
    cst_ref[3] = spread(column_of(along_z[63:64]))
    lane = lax.broadcasted_iota(jnp.int32, (1, LANES), 1)

    def weight(dim):
        own = jnp.where(
            side == 1, coeff_ref[2, pl.ds(patch, 1), :], coeff_ref[0, pl.ds(patch, 1), :]
        )
        shared = coeff_ref[1, pl.ds(patch, 1), :]
        own, shared = (
            jnp.broadcast_to(value[:, dim : dim + 1], (1, LANES)) for value in (own, shared)
        )
        return jnp.where(lane < 64, own, jnp.where(lane < 96, shared, 0.0))

    x_values, y_values, z_values = (values_ref[dim, pl.ds(patch, 1), :] for dim in range(3))
    half_values = jnp.where(side == 1, x_values[:, 32:64], x_values[:, 0:32])
    lane_values = jnp.concatenate([x_values, half_values, half_values], axis=1)
    x_term = jnp.where(lane >= 96, 1.0, weight(0) * lane_values)
    y_term = weight(1) * spread(column_of(y_values))
    cst_ref[4] = x_term + y_term
    cst_ref[5] = weight(2) * spread(column_of(z_values))

    sources = recv_ref.shape[0] // LOAD_ROWS
    load = jnp.concatenate(
        [
            jnp.concatenate(
                [
                    recv_ref[LOAD_ROWS * src + start : LOAD_ROWS * src + start + 8, :]
                    for start in (8 * n, 16 + 8 * n)
                ],
                axis=1,
            )
            for n in range(2)
            for src in range(sources)
        ],
        axis=0,
    )
    fwd_ref[...] = split_dot(bdt_ref, split_dot(bxt_ref, load, 0), 1)

    def step(j, carry):
        top, bottom = carry

        def row(index):
            return jnp.broadcast_to(cst_ref[index, pl.ds(j, 1), :], (64, LANES))

        first = jnp.broadcast_to(fwd_ref[pl.ds(64 + j, 1), :], (64, LANES))
        last = jnp.broadcast_to(fwd_ref[pl.ds(128 + j, 1), :], (64, LANES))
        y_first, y_last = row(0), row(1)
        spectral = (
            y_first * fwd_ref[0:64, :]
            + y_last * fwd_ref[192:256, :]
            + first * cst_ref[2]
            + last * cst_ref[3]
        )
        scaled = spectral / (row(4) + cst_ref[5])
        along_first = cst_ref[2] * scaled
        along_last = cst_ref[3] * scaled
        d0_ref[j] = jnp.sum(along_first.reshape(8, 8, LANES), axis=0)
        d1_ref[j] = jnp.sum(along_last.reshape(8, 8, LANES), axis=0)
        return top + y_first * scaled, bottom + y_last * scaled

    zero = jnp.zeros((64, LANES), F32)
    top, bottom = lax.fori_loop(0, 64, step, (zero, zero), unroll=8)
    edges = jnp.concatenate(
        [top, jnp.sum(d0_ref[...], axis=1), jnp.sum(d1_ref[...], axis=1), bottom], axis=0
    )
    slab_ref[...] = split_dot(bx_ref, split_dot(bd_ref, edges, 0), 1)

    def packed(row):
        halves = []
        for part in range(2):
            starts = [LOAD_ROWS * (4 * part + k) + row for k in range(4)]
            value = recv_ref[starts[0] : starts[0] + 1, :]
            for start in starts[1:]:
                value = value + recv_ref[start : start + 1, :]
            halves.append(value)
        return jnp.concatenate(halves + [jnp.full((6, LANES), -1.0, F32)], axis=0)

    codes = packed(32).astype(jnp.int32)
    ids = packed(33).astype(jnp.int32)
    primal = gather_rows(
        codes,
        lambda a: slab_ref[a % 128 : a % 128 + 1, (a // 128) * LANES : (a // 128 + 1) * LANES],
        256,
    )
    store_digits(ids, high_ref, low_ref)
    for n, piece in enumerate(split_channels(primal, 3)):
        piece_ref[n] = piece
    partial = scatter_small(16, high_ref, low_ref, piece_ref, 2)
    for dest in range(out_ref.shape[0] // SLAB_ROWS):
        base = SLAB_ROWS * dest
        for half in range(2):
            lanes = slice(half * LANES, (half + 1) * LANES)
            for n in range(2):
                start = base + 16 * half + 8 * n
                out_ref[start : start + 8, :] = slab_ref[
                    64 * n + 8 * dest : 64 * n + 8 * dest + 8, lanes
                ]
        out_ref[base + 32 : base + 40, :] = partial[0:8, :]


def pick_kernel(
    recv_ref, idx_ref, small_ref, inv_hbm, out_ref, table_ref, pick_ref, inv_ref, mid_ref,
    lift_ref, flip_ref, high_ref, low_ref, sem,
):
    copy = pltpu.make_async_copy(inv_hbm, inv_ref, sem)
    copy.start()
    sources = recv_ref.shape[0] // SLAB_ROWS

    def block_of(src, start):
        return recv_ref[pl.ds(SLAB_ROWS * src + start, 8), :]

    coarse = block_of(0, 32)
    for src in range(1, sources):
        coarse = coarse + block_of(src, 32)

    def build(p, carry):
        for half in range(2):
            start = pl.multiple_of(p * 48 + half * 24, 8)
            table_ref[pl.ds(start, 8), :] = block_of(2 * p, 16 * half)
            table_ref[pl.ds(start + 8, 8), :] = block_of(2 * p, 16 * half + 8) + block_of(
                2 * p + 1, 16 * half + 8
            )
            table_ref[pl.ds(start + 16, 8), :] = block_of(2 * p + 1, 16 * half)
        return carry

    lax.fori_loop(0, sources // 2, build, 0)
    gather_mixed(idx_ref, table_ref, pick_ref, flip_ref, high_ref, low_ref, 7, 72)
    mid_ref[...] = coarse
    copy.wait()
    coarse_rows = [jnp.broadcast_to(mid_ref[q : q + 1, :], (LANES, LANES)) for q in range(8)]
    ones = jnp.ones((16, LANES), BF16)
    for part in range(8):
        rows = slice(part * LANES, (part + 1) * LANES)
        product = inv_ref[rows, 0:LANES] * coarse_rows[0]
        for q in range(1, 8):
            product = product + inv_ref[rows, q * LANES : (q + 1) * LANES] * coarse_rows[q]
        high, low = split_pair(product)
        lift_ref[part : part + 1, :] = (pair_dot(ones, high) + pair_dot(ones, low))[0:1]
    lift = lift_ref[...]
    mine = own_lanes() == lax.rem(lax.axis_index("group"), 4)
    extra = jnp.where(mine, small_ref[0:2, :], 0.0)
    for h in range(pick_ref.shape[0] // 4):
        start = OWNER_ROWS * h
        out_ref[start : start + 8, :] = lift
        out_ref[start + 8 : start + 12, :] = pick_ref[4 * h : 4 * h + 4, :]
        out_ref[start + 12 : start + 14, :] = extra


def image_kernel(
    own_ref, pair_ref, dir_hbm, res_hbm, scale_hbm, iterate_hbm,
    image_ref, sums_ref, dir_ref, res_ref, scale_ref, iterate_ref,
    lift_ref, high_ref, low_ref, piece_ref, corr_ref, table_ref, flip_ref, pick_ref, wide_high_ref,
    wide_low_ref, sems,
):
    copies = start_copies(
        [
            (dir_hbm, dir_ref),
            (res_hbm, res_ref),
            (scale_hbm, scale_ref),
            (iterate_hbm, iterate_ref),
        ],
        sems,
    )
    groups = own_ref.shape[0] // OWNER_ROWS
    total = own_ref[0:8, :]
    for h in range(1, groups):
        total = total + own_ref[OWNER_ROWS * h : OWNER_ROWS * h + 8, :]
    lift_ref[...] = total

    def packed(row):
        rows = []
        for q in range(8):
            start = OWNER_ROWS * 4 * q + row
            value = own_ref[start : start + 1, :]
            for k in range(1, 4):
                start = OWNER_ROWS * (4 * q + k) + row
                value = value + own_ref[start : start + 1, :]
            rows.append(value)
        return jnp.concatenate(rows, axis=0).astype(jnp.int32)

    local = packed(12) - 512 * lax.axis_index("group")
    ids = packed(13)
    sender = 4 * lax.broadcasted_iota(jnp.int32, (8, LANES), 0) + jnp.broadcast_to(
        own_lanes(), (8, LANES)
    )
    valid = jnp.logical_and(local >= 0, local < 512)
    store_digits(jnp.where(valid, sender * 512 + local, -1), high_ref, low_ref)

    lifted = gather_rows(ids, lambda a: lift_ref[a : a + 1, :], 8)
    for n, piece in enumerate(split_channels(lifted, 3)):
        piece_ref[n] = piece
    corr_ref[...] = scatter_small(4 * groups, high_ref, low_ref, piece_ref, 8)
    for h in range(groups):
        start = OWNER_ROWS * h + 8
        table_ref[4 * h : 4 * h + 4, :] = (
            own_ref[start : start + 4, :] + corr_ref[4 * h : 4 * h + 4, :]
        )
    gather_mixed(pair_ref, table_ref, pick_ref, flip_ref, wide_high_ref, wide_low_ref, 3, 40)
    for copy in copies:
        copy.wait()
    half = dir_ref.shape[0]
    sums = [jnp.zeros((8, LANES), F32) for _ in range(4)]
    for start in range(0, half, 8):
        rows = slice(start, start + 8)
        image = pick_ref[rows, :] - pick_ref[half + start : half + start + 8, :]
        image_ref[rows, :] = image
        scaled = scale_ref[rows, :]
        scaled_res = res_ref[rows, :] * scaled
        sums[0] = sums[0] + scaled_res * res_ref[rows, :]
        sums[1] = sums[1] + dir_ref[rows, :] * image
        sums[2] = sums[2] + scaled_res * image
        sums[3] = sums[3] + (scaled * image) * image
    lane = lax.broadcasted_iota(jnp.int32, (8, LANES), 1)
    packed_sums = jnp.zeros((8, LANES), F32)
    for n, part in enumerate(sums):
        value = jnp.sum(jnp.sum(part, axis=0, keepdims=True), axis=1, keepdims=True)
        packed_sums = jnp.where(lane == n, jnp.broadcast_to(value, (8, LANES)), packed_sums)
    for t in range(sums_ref.shape[0] // 8):
        sums_ref[8 * t : 8 * t + 8, :] = packed_sums


def update_kernel(
    sums_ref, dir_ref, res_ref, scale_ref, iterate_ref, image_ref, it_out, res_out, dir_out
):
    totals = jnp.sum(sums_ref[...], axis=0, keepdims=True)
    lane = lax.broadcasted_iota(jnp.int32, (1, LANES), 1)

    def pick(n):
        return jnp.sum(jnp.where(lane == n, totals, 0.0), axis=1, keepdims=True)

    old, curvature, cross, square = pick(0), pick(1), pick(2), pick(3)
    alpha = old / curvature
    new = old - 2.0 * alpha * cross + (alpha * alpha) * square
    beta = new / old
    direction = dir_ref[...]
    res_next = res_ref[...] - alpha * image_ref[...]
    it_out[...] = iterate_ref[...] + alpha * direction
    res_out[...] = res_next
    dir_out[...] = scale_ref[...] * res_next + beta * direction


def exchange(array, axis):
    return lax.all_to_all(array, axis, split_axis=0, concat_axis=0, tiled=True)


def f32(*shape):
    return jax.ShapeDtypeStruct(shape, F32)


def i32(*shape):
    return jax.ShapeDtypeStruct(shape, jnp.int32)


def body(
    mult_iterate,
    residual,
    direction,
    mult_scale,
    eigen_basis,
    eigen_values,
    elastic_coef,
    coarse_inverse,
    send_pos,
    pair_slots,
    prim_rows,
    coarse_idx,
):
    groups = lax.axis_size("group")
    pencils = lax.axis_size("pencil")
    iterate_now = mult_iterate.reshape(64, LANES)
    resid_now = residual.reshape(64, LANES)
    search_dir = direction.reshape(64, LANES)
    scale_now = mult_scale.reshape(64, LANES)
    cells = send_pos.reshape(128, LANES)
    pairs = pair_slots.reshape(2, 8192)
    primal = prim_rows.reshape(1, 32)
    coarse_ids = coarse_idx.reshape(1, 32)

    def resident(array):
        return pltpu.with_memory_space_constraint(array, pltpu.HBM)

    digits = [pltpu.VMEM((128, LANES), F32), pltpu.VMEM((128, LANES), F32)]
    pieces = pltpu.VMEM((2, 128, LANES), F32)
    small = [
        pltpu.VMEM((8, LANES), F32),
        pltpu.VMEM((8, LANES), F32),
        pltpu.VMEM((3, 8, LANES), F32),
    ]
    sources = (
        pairs,
        search_dir,
        cells,
        primal,
        coarse_ids,
        eigen_basis,
        eigen_values.transpose(1, 0, 2),
        elastic_coef.transpose(1, 0, 2),
    )
    back, pair_rows, cells, primals, *patch_data = call(
        back_kernel,
        (
            f32(128, LANES),
            i32(128, LANES),
            i32(128, LANES),
            f32(8, LANES),
            f32(3, 64, 64),
            f32(3, 4, 64),
            f32(3, 4, 3),
        ),
        [HBM] * len(sources),
        "back",
        [
            pltpu.VMEM((2, 8192), jnp.int32),
            pltpu.VMEM((64, LANES), F32),
            pltpu.VMEM((1, 32), jnp.int32),
            pltpu.VMEM((1, 32), jnp.int32),
        ]
        + digits
        + [pieces, pltpu.VMEM((WIDE, LANES), F32), pltpu.SemaphoreType.DMA((len(sources),))],
    )(*(resident(source) for source in sources))
    arrived = exchange(back.reshape(groups, 4, LANES), "group").reshape(128, LANES)

    loads, slots = call(
        load_kernel,
        (f32(pencils * LOAD_ROWS, LANES), i32(128, LANES)),
        [VMEM] * 3,
        "load",
        digits + [pieces, pltpu.VMEM((192, LANES), F32)],
    )(arrived, cells, primals)
    columns = exchange(loads.reshape(pencils, 1, LOAD_ROWS * LANES), "pencil")

    partial = call(
        solve_kernel,
        f32(pencils * SLAB_ROWS, LANES),
        [VMEM] * 4,
        "solve",
        [
            pltpu.VMEM((128, 384), BF16),
            pltpu.VMEM((128, 384), BF16),
            pltpu.VMEM((256, 768), BF16),
            pltpu.VMEM((256, 768), BF16),
            pltpu.VMEM((6, 64, LANES), F32),
            pltpu.VMEM((256, LANES), F32),
            pltpu.VMEM((64, 8, LANES), F32),
            pltpu.VMEM((64, 8, LANES), F32),
            pltpu.VMEM((128, 256), F32),
        ]
        + small,
    )(columns.reshape(pencils * LOAD_ROWS, LANES), *patch_data)
    slabs = exchange(partial.reshape(pencils, 1, SLAB_ROWS * LANES), "pencil")

    picked = call(
        pick_kernel,
        f32(groups * OWNER_ROWS, LANES),
        [VMEM, VMEM, VMEM, HBM],
        "pick",
        [
            pltpu.VMEM((192, LANES), F32),
            pltpu.VMEM((128, LANES), F32),
            pltpu.VMEM((1024, 1024), F32),
            pltpu.VMEM((8, LANES), F32),
            pltpu.VMEM((8, LANES), F32),
            pltpu.VMEM((LANES, 384), BF16),
        ]
        + digits
        + [
            pltpu.SemaphoreType.DMA,
        ],
    )(slabs.reshape(pencils * SLAB_ROWS, LANES), slots, primals, resident(coarse_inverse))
    owner = exchange(picked.reshape(groups, 1, OWNER_ROWS * LANES), "group")

    shape = f32(64, LANES)
    image, sums, *vectors = call(
        image_kernel,
        (shape, f32(groups * pencils, LANES), shape, shape, shape, shape),
        [VMEM, VMEM] + [HBM] * 4,
        "image",
        [pltpu.VMEM((8, LANES), F32)]
        + small
        + [
            pltpu.VMEM((128, LANES), F32),
            pltpu.VMEM((128, LANES), F32),
            pltpu.VMEM((LANES, 256), BF16),
            pltpu.VMEM((128, LANES), F32),
        ]
        + digits
        + [pltpu.SemaphoreType.DMA((4,))],
    )(
        owner.reshape(groups * OWNER_ROWS, LANES),
        pair_rows,
        *(resident(array) for array in (search_dir, resid_now, scale_now, iterate_now)),
    )
    totals = exchange(sums, ("group", "pencil"))

    outs = call(update_kernel, (shape, shape, shape), [VMEM] * 6, "update")(
        totals, *vectors, image
    )
    return tuple(out.reshape(1, 1, -1) for out in outs)


def solution(mesh):
    in_specs = (
        P("group", "pencil", None),
        P("group", "pencil", None),
        P("group", "pencil", None),
        P("group", "pencil", None),
        P("group", None, None, None),
        P("group", None, None),
        P("group", None, None),
        P(),
        P("group", "pencil", None),
        P("group", "pencil", None, None),
        P("group", "pencil", None),
        P("group", "pencil", None),
    )
    out_specs = (P("group", "pencil", None), P("group", "pencil", None), P("group", "pencil", None))
    return jax.shard_map(body, mesh=mesh, in_specs=in_specs, out_specs=out_specs, check_vma=False)
```
